32 devices in a mesh: atom: 4 (over y, x), row: 2 (over core), col: 4 (over z).
Axes of the slice: x: 2, y: 2, z: 4, core: 2. Of those that a mesh axis runs over, the one named last changes fastest.
Arguments:
- codes: bfloat16 [32, 64, 2048], P('row', 'col', 'atom'), may hold values from -1.5 to 1.5
- image: bfloat16 [32, 64, 128], P('row', 'col'), may hold values from -6 to 6
- master: float32 [128, 7, 7, 2048], P(('row', 'col'), None, None, 'atom'), may hold values from -0.078125 to 0.078125
- moment: float32 [128, 7, 7, 2048], P(('row', 'col'), None, None, 'atom'), may hold values from -120 to 120
- second: float32 [128, 7, 7, 2048], P(('row', 'col'), None, None, 'atom'), may hold values from 100 to 4000
Outputs:
- new_codes: bfloat16 [32, 64, 2048], P('row', 'col', 'atom')
- new_dictionary: float32 [128, 7, 7, 2048], P(('row', 'col'), None, None, 'atom')
- new_moment: float32 [128, 7, 7, 2048], P(('row', 'col'), None, None, 'atom')
- new_second: float32 [128, 7, 7, 2048], P(('row', 'col'), None, None, 'atom')
The draws below stay inside these ranges and needn't reach their ends.
All inputs are finite; a program needn't handle non-finite values.
Results may differ from the reference program's by a relative error of at most 0.007.
Values may be sent and summed in bfloat16 or wider, within the bound.
No kernel may reach another device: no remote copies, remote signals or barrier semaphores. Data moves between devices by JAX's collectives and lax.ppermute only.
A program may use at most 128 MiB of HBM per device.

```python
import math
import jax
import jax.numpy as jnp
from jax import lax

C = 128
K = 2048
FS = 7
NH = 32
NW = 64


def block_scale(stream_key, extent, shards, smallest, high):
    factor_of, own = 1.0, jax.random.fold_in(stream_key, 6)
    for axis_at, parts in shards:
        draws = jnp.exp(jax.random.uniform(jax.random.fold_in(own, axis_at), (parts,), jnp.float32, smallest / len(shards), high / len(shards)))
        factor_of = factor_of * jnp.repeat(draws, extent[axis_at] // parts).reshape([-1 if axis == axis_at else 1 for axis in range(len(extent))])
    return factor_of


def normal_values(rng, dims, spread, bound, pieces=(), dtype=jnp.bfloat16):
    factor_of = block_scale(rng, dims, pieces, -0.22, 0.18) if pieces else 1.0
    drawn = jax.random.normal(rng, dims, jnp.float32) * spread * factor_of
    return jnp.minimum(jnp.maximum(drawn, -bound), bound).astype(dtype)


def setup_inputs(seed: int = 0) -> dict:
    key_of = jax.random.split(jax.random.key(seed), 6)
    codes = normal_values(key_of[0], (NH, NW, K), 0.25, 1.5, ((0, 2), (1, 4), (2, 4)))
    image = normal_values(key_of[1], (NH, NW, C), 1.0, 6.0, ((0, 2), (1, 4)))
    master = normal_values(key_of[2], (C, FS, FS, K), (C * FS * FS) ** -0.5, 0.078125, ((0, 8), (3, 4)), jnp.float32)
    moment = normal_values(key_of[3], (C, FS, FS, K), 20.0, 120.0, ((0, 8), (3, 4)), jnp.float32)
    second = jnp.clip(jnp.exp(math.log(4000.0) - 3.6888795 * jax.random.uniform(key_of[4], (C, FS, FS, K), jnp.float32) ** block_scale(key_of[4], (C, FS, FS, K), ((0, 8), (3, 4)), -0.2, 0.2)), 100.0, 4000.0)
    return {"codes": codes, "image": image, "master": master, "moment": moment, "second": second}


first_fix = 0.9999734386011124
second_fix = 0.09520785288629038

def reference(codes, image, master, moment, second):
    rows_all, cols_all, atoms = codes.shape
    bands = image.shape[2]
    pixels = rows_all * cols_all
    filters = master.astype(jnp.bfloat16)
    zero = jnp.zeros((), jnp.int32)
    code_pad = jnp.pad(codes, ((3, 3), (3, 3), (0, 0)))

    def add_synth(tap_index, total):
        tap_row = (tap_index // FS).astype(jnp.int32)
        tap_col = (tap_index % FS).astype(jnp.int32)
        window = lax.dynamic_slice(code_pad, (tap_row, tap_col, zero), (rows_all, cols_all, atoms)).reshape(pixels, atoms)
        tap = lax.dynamic_slice(filters, (zero, tap_row, tap_col, zero), (bands, 1, 1, atoms)).reshape(bands, atoms)
        return total + jnp.dot(window, tap.T, preferred_element_type=jnp.float32)
    synth = lax.fori_loop(0, FS * FS, add_synth, jnp.zeros((pixels, bands), jnp.float32))
    resid = (synth - image.reshape(pixels, bands).astype(jnp.float32)).astype(jnp.bfloat16)
    resid_pad = jnp.pad(resid.reshape(rows_all, cols_all, bands), ((3, 3), (3, 3), (0, 0)))

    def add_both(tap_index, carry):
        back, grad = carry
        tap_row = (tap_index // FS).astype(jnp.int32)
        tap_col = (tap_index % FS).astype(jnp.int32)
        tap = lax.dynamic_slice(filters, (zero, tap_row, tap_col, zero), (bands, 1, 1, atoms)).reshape(bands, atoms)
        flipped = lax.dynamic_slice(resid_pad, (6 - tap_row, 6 - tap_col, zero), (rows_all, cols_all, bands)).reshape(pixels, bands)
        back = back + jnp.dot(flipped, tap, preferred_element_type=jnp.float32)
        window = lax.dynamic_slice(code_pad, (tap_row, tap_col, zero), (rows_all, cols_all, atoms)).reshape(pixels, atoms)
        term = lax.dot_general(resid, window, (((0,), (0,)), ((), ())), preferred_element_type=jnp.float32)
        grad = lax.dynamic_update_slice(grad, term.reshape(bands, 1, 1, atoms), (zero, tap_row, tap_col, zero))
        return (back, grad)
    back, grad = lax.fori_loop(0, FS * FS, add_both, (jnp.zeros((pixels, atoms), jnp.float32), jnp.zeros((bands, FS, FS, atoms), jnp.float32)))
    moved = codes.reshape(pixels, atoms).astype(jnp.float32) - 0.05 * back
    new_codes = (moved - jnp.clip(moved, -0.02, 0.02)).astype(jnp.bfloat16).reshape(rows_all, cols_all, atoms)
    new_moment = 0.9 * moment + 0.1 * grad
    new_second = 0.999 * second + 0.001 * grad * grad
    new_dictionary = master - 0.05 * (new_moment / first_fix) / (jnp.sqrt(new_second / second_fix) + 1e-08)
    return (new_codes, new_dictionary, new_moment, new_second)
```

```python
import functools

import jax
import jax.numpy as jnp
from jax import lax
from jax.experimental import pallas as pl
from jax.experimental.pallas import tpu as pltpu
from jax.sharding import PartitionSpec as P

first_fix = 0.9999734386011124
second_fix = 0.09520785288629038


def shifted(x, axis, step):
    count = lax.axis_size(axis)
    return lax.ppermute(x, axis, [(i, (i + step) % count) for i in range(count)])


def moved_on(x, axis, step):
    count = lax.axis_size(axis)
    return lax.ppermute(x, axis, [(i, i + step) for i in range(count) if 0 <= i + step < count])


def whole(count, *extra):
    return [pl.BlockSpec(memory_space=pltpu.VMEM)] * count + list(extra)


def call(body, outs, args, flops=0, scratch=(), name=None):
    moved = sum(a.size * a.dtype.itemsize for a in args) + sum(o.size * o.dtype.itemsize for o in outs)
    return pl.pallas_call(
        body,
        out_shape=outs,
        in_specs=whole(len(args)),
        out_specs=whole(len(outs)),
        scratch_shapes=list(scratch),
        cost_estimate=pl.CostEstimate(flops=flops, bytes_accessed=moved, transcendentals=0),
        compiler_params=pltpu.CompilerParams(vmem_limit_bytes=60 << 20),
        name=name,
    )(*args)


def roll(x, amount):
    amount %= x.shape[1]
    return pltpu.roll(x, amount, 1) if amount else x


def struct(shape, dtype):
    return jax.ShapeDtypeStruct(shape, dtype)


def column_of(ext, cols):
    return lax.broadcasted_iota(jnp.int32, (1, ext), 1) % cols


def tile_parts(filters, tile, y_ref, taps, bands, ext, cols):
    reach = taps // 2
    y_ref[...] = lax.dot_general(filters, tile, (((1,), (1,)), ((), ())), preferred_element_type=jnp.float32)
    pixels = tile.shape[0]
    column = column_of(ext, cols)
    main = jnp.zeros((bands, ext), jnp.float32)
    to_right = jnp.zeros((bands, ext), jnp.float32)
    to_left = jnp.zeros((bands, ext), jnp.float32)
    tail = jnp.zeros((bands, ext - pixels), jnp.float32)
    for b in range(taps):
        total = None
        for a in range(taps):
            term = jnp.concatenate([y_ref[pl.ds((a * taps + b) * bands, bands), :], tail], axis=1)
            total = term if total is None else roll(total, cols) + term
        step = reach - b
        turned = roll(total, step)
        if step > 0:
            inside = column >= step
            to_right = to_right + jnp.where(inside, 0.0, turned)
        elif step < 0:
            inside = column < cols + step
            to_left = to_left + jnp.where(inside, 0.0, turned)
        main = main + (turned if step == 0 else jnp.where(inside, turned, 0.0))
    return main, roll(to_right, -cols) + roll(to_left, cols)


def early_body(taps, bands, ext, cols, filters_ref, tile_ref, main_ref, spill_ref, y_ref):
    main, spill = tile_parts(filters_ref[...], tile_ref[...], y_ref, taps, bands, ext, cols)
    main_ref[...] = main
    spill_ref[...] = spill


def tile_flags(axis, s):
    count = lax.axis_size(axis)
    place = lax.rem(lax.axis_index(axis) + count - s, count)
    return place > 0, place < count - 1


def late_body(taps, bands, ext, cols, order, share, *refs):
    count = len(order) + 1
    filters_ref, tile_ref = refs[:2]
    mains, spills = refs[2 : 2 + count - 1], refs[1 + count : 2 * count]
    images = refs[2 * count : 3 * count]
    out_ref, y_ref = refs[3 * count], refs[3 * count + 1]
    reach = taps // 2
    main, spill = tile_parts(filters_ref[...], tile_ref[...], y_ref, taps, bands, ext, cols)
    last = (set(range(count)) - set(order)).pop()
    main_of, spill_of = {last: main}, {last: spill}
    for place, s in enumerate(order):
        main_of[s] = mains[place][...]
        spill_of[s] = spills[place][...]
    column = column_of(ext, cols)
    for s in range(count):
        left, right = tile_flags("col", s)
        from_left = jnp.where((column < reach) & left, spill_of[(s + 1) % count], 0.0)
        from_right = jnp.where((column >= cols - reach) & right, spill_of[(s - 1) % count], 0.0)
        picture = images[s][...].astype(jnp.float32) * share
        pad = jnp.zeros((bands, ext - picture.shape[1]), jnp.float32)
        picture = roll(jnp.concatenate([picture, pad], axis=1), reach * cols)
        out_ref[:, s * ext : (s + 1) * ext] = main_of[s] + from_left + from_right - picture


def edges_body(count, ext, pixels, edge, z_ref, up_ref, down_ref):
    lane = lax.broadcasted_iota(jnp.int32, (1, 128), 1)
    for s in range(count):
        up_ref[:, s * 128 : (s + 1) * 128] = jnp.where(lane < edge, z_ref[:, s * ext : s * ext + 128], 0.0)
        down_ref[:, s * 128 : (s + 1) * 128] = z_ref[:, s * ext + pixels : s * ext + pixels + 128]


def join_body(count, ext, pixels, turn, z_ref, below_ref, above_ref, out_ref, send_ref):
    bands = z_ref.shape[0]

    def turned(x, step):
        step %= bands
        return x if step == 0 else jnp.concatenate([x[bands - step :], x[: bands - step]], axis=0)

    for s in range(count):
        at = s * ext
        own = z_ref[:, at : at + ext]
        above = turned(above_ref[:, s * 128 : (s + 1) * 128], turn)
        below = turned(below_ref[:, s * 128 : (s + 1) * 128], -turn)
        out_ref[:, at : at + 128] = own[:, :128] + above
        out_ref[:, at + 128 : at + pixels] = own[:, 128:pixels]
        out_ref[:, at + pixels : at + pixels + 128] = own[:, pixels : pixels + 128] + below
        if pixels + 128 < ext:
            out_ref[:, at + pixels + 128 : at + ext] = own[:, pixels + 128 :]
    send_ref[...] = out_ref[...].astype(jnp.bfloat16)


def resid_windows(taps, bands, ext, rows, cols, count, total, windows_ref):
    reach = taps // 2
    pixels = rows * cols
    line = lax.broadcasted_iota(jnp.int32, (1, ext), 1) // cols
    column = column_of(ext, cols)
    place, places = lax.axis_index("row"), lax.axis_size("row")
    real = ((line >= reach) | (place > 0)) & ((line < rows + reach) | (place < places - 1)) & (line < rows + 2 * reach)
    tiles = [jnp.where(real, total(s), 0.0).astype(jnp.bfloat16).astype(jnp.float32) for s in range(count)]
    for s in range(count):
        left, right = tile_flags("col", s)
        own = tiles[s]
        to_left = jnp.where(left, tiles[(s + 1) % count], 0.0)
        to_right = jnp.where(right, tiles[(s - 1) % count], 0.0)
        for b in range(taps):
            step = b - reach
            if step == 0:
                view = own
            elif step > 0:
                view = jnp.where(column >= step, roll(own, step), roll(to_left, step - cols))
            else:
                view = jnp.where(column < cols + step, roll(own, step), roll(to_right, step + cols))
            for a in range(taps):
                part = roll(view, -cols * (2 * reach - a))[:, :pixels]
                at = (a * taps + b) * bands
                windows_ref[at : at + bands, s * pixels : (s + 1) * pixels] = part.astype(jnp.bfloat16)


def back_body(taps, bands, ext, rows, cols, count, peers, *refs):
    turned_ref, own_ref = refs[:2]
    others = refs[2 : 2 + peers]
    windows_ref = refs[2 + peers]
    outs = refs[3 + peers :]
    pixels = rows * cols

    def total(s):
        value = own_ref[:, s * ext : (s + 1) * ext]
        for other in others:
            value = value + other[:, s * ext : (s + 1) * ext].astype(jnp.float32)
        return value

    resid_windows(taps, bands, ext, rows, cols, count, total, windows_ref)
    for s in range(1, count):
        outs[s - 1][...] = jnp.dot(
            turned_ref[...], windows_ref[:, s * pixels : (s + 1) * pixels], preferred_element_type=jnp.float32
        ).astype(jnp.bfloat16)


def grad_body(count, pixels, *refs):
    windows_ref, turned_ref = refs[:2]
    tiles = refs[2 : 2 + count]
    back_ref, grad_ref = refs[2 + count :]
    total = None
    for s in range(count):
        term = jnp.dot(windows_ref[:, s * pixels : (s + 1) * pixels], tiles[s][...], preferred_element_type=jnp.float32)
        total = term if total is None else total + term
    grad_ref[...] = total
    back_ref[...] = jnp.dot(turned_ref[...], windows_ref[:, :pixels], preferred_element_type=jnp.float32)


def codes_body(*refs):
    codes_ref, back_ref = refs[:2]
    others, out_ref = refs[2:-1], refs[-1]
    back = back_ref[...]
    for other in others:
        back = back + other[...].astype(jnp.float32)
    moved = codes_ref[...].astype(jnp.float32) - 0.05 * back.T
    out_ref[...] = (moved - jnp.clip(moved, -0.02, 0.02)).astype(jnp.bfloat16)


def adam_update(master, moment, second, grad):
    new_moment = 0.9 * moment + 0.1 * grad
    new_second = 0.999 * second + 0.001 * grad * grad
    new_dictionary = master - 0.05 * (new_moment / first_fix) / (
        jnp.sqrt(new_second / second_fix) + 1e-08
    )
    return (new_dictionary, new_moment, new_second)


def local(codes, image, master, moment, second):
    rows, cols, atoms = codes.shape
    own_bands, taps = master.shape[0], master.shape[1]
    groups, count, peers = lax.axis_size("row"), lax.axis_size("col"), lax.axis_size("atom")
    bands = groups * own_bands
    reach = taps // 2
    pixels = rows * cols
    ext = -(-(rows + 2 * reach) * cols // 128) * 128
    row_at, col_at = lax.axis_index("row"), lax.axis_index("col")

    order = sorted(range(1, count), key=lambda s: (abs(count - 2 * s), s))
    tiles = {0: codes.reshape(pixels, atoms)}
    for s in order:
        tiles[s] = shifted(codes, "col", s).reshape(pixels, atoms)

    own_filters = jnp.transpose(master, (1, 2, 0, 3)).reshape(taps * taps, own_bands, atoms).astype(jnp.bfloat16)
    filters = jnp.concatenate([own_filters] + [shifted(own_filters, "row", s) for s in range(1, groups)], axis=1)
    filters = filters.reshape(taps * taps * bands, atoms)
    turned = filters.T

    picture = image.reshape(pixels, groups, count, own_bands).transpose(1, 2, 3, 0)
    picture = jnp.stack([lax.dynamic_index_in_dim(picture, (row_at + groups - s) % groups, 0, False) for s in range(groups)])
    images = []
    for s in range(count):
        piece = lax.dynamic_index_in_dim(picture, (col_at + s) % count, 1, False).reshape(bands, pixels)
        images.append(piece if s == 0 else shifted(piece, "col", s))

    size = (bands, ext)
    y_scratch = [pltpu.VMEM((taps * taps * bands, pixels), jnp.float32)]
    tile_flops = 2 * taps * taps * bands * pixels * atoms
    mains, spills = [], []
    early = [0] + order[:-1]
    for s in early:
        main, spill = call(
            functools.partial(early_body, taps, bands, ext, cols),
            [struct(size, jnp.float32)] * 2,
            [filters, tiles[s]],
            tile_flops,
            y_scratch,
            "synth_early",
        )
        mains.append(main)
        spills.append(spill)
    share = 1.0 / peers
    (part,) = call(
        functools.partial(late_body, taps, bands, ext, cols, tuple(early), share),
        [struct((bands, count * ext), jnp.float32)],
        [filters, tiles[order[-1]], *mains, *spills, *images],
        tile_flops,
        y_scratch,
        "synth_late",
    )
    edge = struct((bands, count * 128), jnp.float32)
    up, down = call(functools.partial(edges_body, count, ext, pixels, 2 * reach * cols), [edge, edge], [part], name="edges")
    below = moved_on(up, "row", -1)
    above = moved_on(down, "row", 1)
    part, send = call(
        functools.partial(join_body, count, ext, pixels, own_bands),
        [struct(part.shape, jnp.float32), struct(part.shape, jnp.bfloat16)],
        [part, below, above],
        name="join",
    )
    if peers <= 4:
        others = [lax.ppermute(send, "atom", [(i, i ^ m) for i in range(peers)]) for m in range(peers - 1, 0, -1)]
    else:
        others = [(lax.psum(send, "atom").astype(jnp.float32) - send.astype(jnp.float32)).astype(jnp.bfloat16)]

    back_shape = struct((atoms, pixels), jnp.bfloat16)
    windows, *backs = call(
        functools.partial(back_body, taps, bands, ext, rows, cols, count, len(others)),
        [struct((taps * taps * bands, count * pixels), jnp.bfloat16)] + [back_shape] * (count - 1),
        [turned, part, *others],
        tile_flops * (count - 1),
        name="back",
    )
    received = [shifted(backs[s - 1], "col", -s) for s in order]
    own_back, grad = call(
        functools.partial(grad_body, count, pixels),
        [struct((atoms, pixels), jnp.float32), struct((taps * taps * bands, atoms), jnp.float32)],
        [windows, turned] + [tiles[s] for s in range(count)],
        tile_flops * (count + 1),
        name="grad",
    )
    grad = grad.reshape(taps * taps, groups, own_bands, atoms)
    own_grad = grad[:, 0]
    for s in range(1, groups):
        own_grad = own_grad + shifted(grad[:, s].astype(jnp.bfloat16), "row", -s).astype(jnp.float32)
    own_grad = jnp.transpose(own_grad.reshape(taps, taps, own_bands, atoms), (2, 0, 1, 3))
    new_dictionary, new_moment, new_second = adam_update(master, moment, second, own_grad)
    (new_codes,) = call(
        codes_body,
        [struct((pixels, atoms), jnp.bfloat16)],
        [codes.reshape(pixels, atoms), own_back, *received],
        name="shrink",
    )
    return (new_codes.reshape(rows, cols, atoms), new_dictionary, new_moment, new_second)


def solution(mesh):
    return jax.shard_map(
        local,
        mesh=mesh,
        in_specs=(
            P("row", "col", "atom"),
            P("row", "col", None),
            P(("row", "col"), None, None, "atom"),
            P(("row", "col"), None, None, "atom"),
            P(("row", "col"), None, None, "atom"),
        ),
        out_specs=(
            P("row", "col", "atom"),
            P(("row", "col"), None, None, "atom"),
            P(("row", "col"), None, None, "atom"),
            P(("row", "col"), None, None, "atom"),
        ),
        check_vma=False,
    )
```

```python
import functools

import jax
import jax.numpy as jnp
from jax import lax
from jax.experimental import pallas as pl
from jax.experimental.pallas import tpu as pltpu
from jax.sharding import PartitionSpec as P


first_fix = 0.9999734386011124
second_fix = 0.09520785288629038


def shifted(x, axis, step):
    count = lax.axis_size(axis)
    return lax.ppermute(x, axis, [(i, (i + step) % count) for i in range(count)])


def moved_on(x, axis, step):
    count = lax.axis_size(axis)
    return lax.ppermute(x, axis, [(i, i + step) for i in range(count) if 0 <= i + step < count])


def call(body, outs, args, flops=0, scratch=()):
    moved = sum(a.size * a.dtype.itemsize for a in args) + sum(o.size * o.dtype.itemsize for o in outs)
    return pl.pallas_call(
        body,
        out_shape=outs,
        in_specs=[pl.BlockSpec(memory_space=pltpu.VMEM)] * len(args),
        out_specs=[pl.BlockSpec(memory_space=pltpu.VMEM)] * len(outs),
        scratch_shapes=list(scratch),
        cost_estimate=pl.CostEstimate(flops=flops, bytes_accessed=moved, transcendentals=0),
        compiler_params=pltpu.CompilerParams(vmem_limit_bytes=24 << 20),
    )(*args)


def roll(x, amount):
    amount %= x.shape[1]
    return pltpu.roll(x, amount, 1) if amount else x


def struct(shape, dtype):
    return jax.ShapeDtypeStruct(shape, dtype)


def column_of(ext, cols):
    return lax.broadcasted_iota(jnp.int32, (1, ext), 1) % cols


def tile_parts(filters, tile, y_ref, taps, bands, ext, cols):
    reach = taps // 2
    y_ref[...] = lax.dot_general(filters, tile, (((1,), (1,)), ((), ())), preferred_element_type=jnp.float32)
    pixels = tile.shape[0]
    column = column_of(ext, cols)
    main = jnp.zeros((bands, ext), jnp.float32)
    to_right = jnp.zeros((bands, ext), jnp.float32)
    to_left = jnp.zeros((bands, ext), jnp.float32)
    tail = jnp.zeros((bands, ext - pixels), jnp.float32)
    for b in range(taps):
        total = None
        for a in range(taps):
            term = jnp.concatenate([y_ref[pl.ds((a * taps + b) * bands, bands), :], tail], axis=1)
            total = term if total is None else roll(total, cols) + term
        step = reach - b
        turned = roll(total, step)
        if step > 0:
            inside = column >= step
            to_right = to_right + jnp.where(inside, 0.0, turned)
        elif step < 0:
            inside = column < cols + step
            to_left = to_left + jnp.where(inside, 0.0, turned)
        main = main + (turned if step == 0 else jnp.where(inside, turned, 0.0))
    return main, roll(to_right, -cols) + roll(to_left, cols)


def early_body(taps, bands, ext, cols, filters_ref, tile_ref, main_ref, spill_ref, y_ref):
    main, spill = tile_parts(filters_ref[...], tile_ref[...], y_ref, taps, bands, ext, cols)
    main_ref[...] = main
    spill_ref[...] = spill


def tile_flags(axis, s):
    count = lax.axis_size(axis)
    place = lax.rem(lax.axis_index(axis) + count - s, count)
    return place > 0, place < count - 1


def late_body(taps, bands, ext, cols, pixels, order, share, *refs):
    count = len(order) + 1
    filters_ref, tile_ref = refs[:2]
    mains, spills = refs[2 : 1 + count], refs[1 + count : 2 * count]
    images = refs[2 * count : 3 * count]
    out_ref, *edge_refs, y_ref = refs[3 * count :]
    reach = taps // 2
    main, spill = tile_parts(filters_ref[...], tile_ref[...], y_ref, taps, bands, ext, cols)
    last = (set(range(count)) - set(order)).pop()
    main_of, spill_of = {last: main}, {last: spill}
    for place, s in enumerate(order):
        main_of[s] = mains[place][...]
        spill_of[s] = spills[place][...]
    column = column_of(ext, cols)
    lane = lax.broadcasted_iota(jnp.int32, (1, 128), 1)
    for s in range(count):
        left, right = tile_flags("col", s)
        from_left = jnp.where((column < reach) & left, spill_of[(s + 1) % count], 0.0)
        from_right = jnp.where((column >= cols - reach) & right, spill_of[(s - 1) % count], 0.0)
        picture = images[s][...].astype(jnp.float32) * share
        pad = jnp.zeros((bands, ext - picture.shape[1]), jnp.float32)
        picture = roll(jnp.concatenate([picture, pad], axis=1), reach * cols)
        value = main_of[s] + from_left + from_right - picture
        out_ref[:, s * ext : (s + 1) * ext] = value
        up = jnp.where(lane < 2 * reach * cols, value[:, :128], 0.0)
        down = value[:, pixels : pixels + 128]
        if len(edge_refs) == 1:
            edges = [jnp.where(lax.axis_index("row") == 0, down, up)]
        else:
            edges = [up, down]
        for ref, edge in zip(edge_refs, edges):
            ref[:, s * 128 : (s + 1) * 128] = edge


def join_body(count, ext, pixels, turn, *refs):
    part_ref, *edge_refs, out_ref, send_ref = refs
    bands = part_ref.shape[0]

    def turned(x, step):
        step %= bands
        return x if step == 0 else jnp.concatenate([x[bands - step :], x[: bands - step]], axis=0)

    for s in range(count):
        at = s * ext
        pieces = [turned(ref[:, s * 128 : (s + 1) * 128], turn * sign) for ref, sign in zip(edge_refs, (-1, 1))]
        if len(pieces) == 1:
            first = lax.axis_index("row") == 0
            pieces = [jnp.where(first, pieces[0], 0.0), jnp.where(first, 0.0, pieces[0])]
        below, above = pieces
        own = part_ref[:, at : at + ext]
        parts = [own[:, :128] + above, own[:, 128:pixels], own[:, pixels : pixels + 128] + below, own[:, pixels + 128 :]]
        value = jnp.concatenate([part for part in parts if part.shape[1]], axis=1)
        out_ref[:, at : at + ext] = value
        send_ref[:, at : at + ext] = value.astype(jnp.bfloat16)


def resid_body(ext, rows, cols, count, reach, peers, *refs):
    own_ref, others, out_ref = refs[0], refs[1 : 1 + peers], refs[1 + peers]
    line = lax.broadcasted_iota(jnp.int32, (1, ext), 1) // cols
    place, places = lax.axis_index("row"), lax.axis_size("row")
    real = ((line >= reach) | (place > 0)) & ((line < rows + reach) | (place < places - 1)) & (line < rows + 2 * reach)
    for s in range(count):
        value = own_ref[:, s * ext : (s + 1) * ext]
        for other in others:
            value = value + other[:, s * ext : (s + 1) * ext].astype(jnp.float32)
        out_ref[:, s * ext : (s + 1) * ext] = jnp.where(real, value, 0.0).astype(jnp.bfloat16).astype(jnp.float32)


def windows_of(taps, bands, ext, rows, cols, count, s, resid_ref, windows_ref):
    reach = taps // 2
    pixels = rows * cols
    column = column_of(ext, cols)

    def tile(s):
        return resid_ref[:, s * ext : (s + 1) * ext]

    left, right = tile_flags("col", s)
    own = tile(s)
    to_left = jnp.where(left, tile((s + 1) % count), 0.0)
    to_right = jnp.where(right, tile((s - 1) % count), 0.0)
    for b in range(taps):
        step = b - reach
        if step == 0:
            view = own
        elif step > 0:
            view = jnp.where(column >= step, roll(own, step), roll(to_left, step - cols))
        else:
            view = jnp.where(column < cols + step, roll(own, step), roll(to_right, step + cols))
        for a in range(taps):
            part = roll(view, -cols * (2 * reach - a))[:, :pixels]
            at = (a * taps + b) * bands
            windows_ref[at : at + bands, :] = part.astype(jnp.bfloat16)


def back_body(taps, bands, ext, rows, cols, count, s, peers, *refs):
    turned_ref = refs[0]
    if peers is None:
        resid_ref, (windows_ref, back_ref) = refs[1], refs[2:]
    else:
        windows_ref, back_ref, resid_ref = refs[-3:]
        resid_body(ext, rows, cols, count, taps // 2, peers, *refs[1:-3], resid_ref)
    windows_of(taps, bands, ext, rows, cols, count, s, resid_ref, windows_ref)
    back = jnp.dot(turned_ref[...], windows_ref[...], preferred_element_type=jnp.float32)
    back_ref[...] = back.astype(back_ref.dtype)


def grad_body(count, *refs):
    windows, tiles, grad_ref = refs[:count], refs[count : 2 * count], refs[2 * count]
    total = None
    for s in range(count):
        term = jnp.dot(windows[s][...], tiles[s][...], preferred_element_type=jnp.float32)
        total = term if total is None else total + term
    grad_ref[...] = total


def codes_body(*refs):
    codes_ref, back_ref = refs[:2]
    others, out_ref = refs[2:-1], refs[-1]
    back = back_ref[...]
    for other in others:
        back = back + other[...].astype(jnp.float32)
    moved = codes_ref[...].astype(jnp.float32) - 0.05 * back.T
    out_ref[...] = (moved - jnp.clip(moved, -0.02, 0.02)).astype(jnp.bfloat16)


def adam_update(master, moment, second, grad):
    new_moment = 0.9 * moment + 0.1 * grad
    new_second = 0.999 * second + 0.001 * grad * grad
    new_dictionary = master - 0.05 * (new_moment / first_fix) / (
        jnp.sqrt(new_second / second_fix) + 1e-08
    )
    return (new_dictionary, new_moment, new_second)


def iteration(codes, image, master, moment, second):
    rows, cols, atoms = codes.shape
    own_bands, taps = master.shape[0], master.shape[1]
    groups, count, peers = lax.axis_size("row"), lax.axis_size("col"), lax.axis_size("atom")
    bands = groups * own_bands
    reach = taps // 2
    pixels = rows * cols
    ext = -(-(rows + 2 * reach) * cols // 128) * 128
    row_at, col_at = lax.axis_index("row"), lax.axis_index("col")

    order = column_order(count)
    tiles = {0: codes.reshape(pixels, atoms)}
    for s in order:
        tiles[s] = shifted(codes, "col", s).reshape(pixels, atoms)

    own_filters = jnp.transpose(master, (1, 2, 0, 3)).reshape(taps * taps, own_bands, atoms).astype(jnp.bfloat16)
    filters = [own_filters]
    for s in range(1, groups):
        filters.append(shifted(own_filters, "row", s))
    filters = jnp.concatenate(filters, axis=1).reshape(taps * taps * bands, atoms)
    turned = filters.T

    picture = image.reshape(pixels, groups, count, own_bands).transpose(1, 2, 3, 0)
    picture = jnp.stack([lax.dynamic_index_in_dim(picture, (row_at + groups - s) % groups, 0, False) for s in range(groups)])
    pieces = [lax.dynamic_index_in_dim(picture, (col_at + s) % count, 1, False).reshape(bands, pixels) for s in range(count)]
    images = []
    for s in range(count):
        images.append(pieces[s] if s == 0 else shifted(pieces[s], "col", s))

    size = struct((bands, ext), jnp.float32)
    y_scratch = [pltpu.VMEM((taps * taps * bands, pixels), jnp.float32)]
    tile_flops = 2 * taps * taps * bands * pixels * atoms
    mains, spills = [], []
    early = [0] + order[:-1]
    for s in early:
        body = functools.partial(early_body, taps, bands, ext, cols)
        main, spill = call(body, [size, size], [filters, tiles[s]], tile_flops, y_scratch)
        mains.append(main)
        spills.append(spill)
    edge = struct((bands, count * 128), jnp.float32)
    part, *edges = call(
        functools.partial(late_body, taps, bands, ext, cols, pixels, tuple(early), 1.0 / peers),
        [struct((bands, count * ext), jnp.float32)] + [edge] * (1 if groups == 2 else 2),
        [filters, tiles[order[-1]], *mains, *spills, *images],
        tile_flops,
        y_scratch,
    )
    if groups == 2:
        edges = [shifted(edges[0], "row", 1)]
    else:
        edges = [moved_on(edges[0], "row", -1), moved_on(edges[1], "row", 1)]
    part, send = call(
        functools.partial(join_body, count, ext, pixels, own_bands),
        [struct(part.shape, jnp.float32), struct(part.shape, jnp.bfloat16)],
        [part, *edges],
    )
    if peers <= 4:
        others = []
        for m in range(peers - 1, 0, -1):
            others.append(lax.ppermute(send, "atom", [(i, i ^ m) for i in range(peers)]))
    else:
        others = [(lax.psum(send, "atom").astype(jnp.float32) - send.astype(jnp.float32)).astype(jnp.bfloat16)]

    windows, received = {}, []
    for place, s in enumerate(order + [0]):
        body = functools.partial(
            back_body, taps, bands, ext, rows, cols, count, s, len(others) if place == 0 else None
        )
        outs = [
            struct((taps * taps * bands, pixels), jnp.bfloat16),
            struct((atoms, pixels), jnp.bfloat16 if s else jnp.float32),
        ]
        if place == 0:
            windows[s], back, resid = call(
                body, outs + [struct(part.shape, jnp.float32)], [turned, part, *others], tile_flops
            )
        else:
            windows[s], back = call(body, outs, [turned, resid], tile_flops)
        if s:
            received.append(shifted(back, "col", -s))
    own_back = back
    (grad,) = call(
        functools.partial(grad_body, count),
        [struct((taps * taps * bands, atoms), jnp.float32)],
        [windows[s] for s in range(count)] + [tiles[s] for s in range(count)],
        tile_flops * count,
    )
    grad = grad.reshape(taps * taps, groups, own_bands, atoms)
    own_grad = grad[:, 0]
    for s in range(1, groups):
        piece = grad[:, s].astype(jnp.bfloat16)
        piece = shifted(piece, "row", -s)
        own_grad = own_grad + piece.astype(jnp.float32)
    own_grad = jnp.transpose(own_grad.reshape(taps, taps, own_bands, atoms), (2, 0, 1, 3))
    new_dictionary, new_moment, new_second = adam_update(master, moment, second, own_grad)
    (new_codes,) = call(
        codes_body, [struct((pixels, atoms), jnp.bfloat16)], [codes.reshape(pixels, atoms), own_back, *received]
    )
    return (new_codes.reshape(rows, cols, atoms), new_dictionary, new_moment, new_second)


def column_order(count):
    return sorted(range(1, count), key=lambda s: (abs(count - 2 * s), s))


def solution(mesh):
    return jax.shard_map(
        iteration,
        mesh=mesh,
        in_specs=(
            P("row", "col", "atom"),
            P("row", "col", None),
            P(("row", "col"), None, None, "atom"),
            P(("row", "col"), None, None, "atom"),
            P(("row", "col"), None, None, "atom"),
        ),
        out_specs=(
            P("row", "col", "atom"),
            P(("row", "col"), None, None, "atom"),
            P(("row", "col"), None, None, "atom"),
            P(("row", "col"), None, None, "atom"),
        ),
        check_vma=False,
    )
```

```python
import functools

import jax
import jax.numpy as jnp
from jax import lax
from jax.experimental import pallas as pl
from jax.experimental.pallas import tpu as pltpu
from jax.sharding import PartitionSpec as P


first_fix = 0.9999734386011124
second_fix = 0.09520785288629038


def shifted(x, axis, step):
    count = lax.axis_size(axis)
    return lax.ppermute(x, axis, [(i, (i + step) % count) for i in range(count)])


def moved_on(x, axis, step):
    count = lax.axis_size(axis)
    return lax.ppermute(x, axis, [(i, i + step) for i in range(count) if 0 <= i + step < count])


TWO = [(0, 2), (1, 3), (2, 0), (3, 1)]
NEAR = [(0, 1), (1, 0), (2, 3), (3, 2)]
INNER = [(1, 2), (2, 1)]


def along(x, pairs):
    return lax.ppermute(x, "col", pairs)


def call(body, outs, args, flops=0, scratch=()):
    moved = sum(a.size * a.dtype.itemsize for a in args) + sum(o.size * o.dtype.itemsize for o in outs)
    return pl.pallas_call(
        body,
        out_shape=outs,
        in_specs=[pl.BlockSpec(memory_space=pltpu.VMEM)] * len(args),
        out_specs=[pl.BlockSpec(memory_space=pltpu.VMEM)] * len(outs),
        scratch_shapes=list(scratch),
        cost_estimate=pl.CostEstimate(flops=flops, bytes_accessed=moved, transcendentals=0),
        compiler_params=pltpu.CompilerParams(vmem_limit_bytes=24 << 20),
    )(*args)


def roll(x, amount):
    amount %= x.shape[1]
    return pltpu.roll(x, amount, 1) if amount else x


def struct(shape, dtype):
    return jax.ShapeDtypeStruct(shape, dtype)


def column_of(ext, cols):
    return lax.broadcasted_iota(jnp.int32, (1, ext), 1) % cols


def tile_parts(filters, tile, y_ref, taps, bands, ext, cols):
    reach = taps // 2
    y_ref[...] = lax.dot_general(filters, tile, (((1,), (1,)), ((), ())), preferred_element_type=jnp.float32)
    pixels = tile.shape[0]
    column = column_of(ext, cols)
    main = jnp.zeros((bands, ext), jnp.float32)
    to_right = jnp.zeros((bands, ext), jnp.float32)
    to_left = jnp.zeros((bands, ext), jnp.float32)
    tail = jnp.zeros((bands, ext - pixels), jnp.float32)
    for b in range(taps):
        total = None
        for a in range(taps):
            term = jnp.concatenate([y_ref[pl.ds((a * taps + b) * bands, bands), :], tail], axis=1)
            total = term if total is None else roll(total, cols) + term
        step = reach - b
        turned = roll(total, step)
        if step > 0:
            inside = column >= step
            to_right = to_right + jnp.where(inside, 0.0, turned)
        elif step < 0:
            inside = column < cols + step
            to_left = to_left + jnp.where(inside, 0.0, turned)
        main = main + (turned if step == 0 else jnp.where(inside, turned, 0.0))
    return main, roll(to_right, -cols) + roll(to_left, cols)


def early_body(taps, bands, ext, cols, filters_ref, tile_ref, main_ref, spill_ref, y_ref):
    main, spill = tile_parts(filters_ref[...], tile_ref[...], y_ref, taps, bands, ext, cols)
    main_ref[...] = main
    spill_ref[...] = spill


def tile_flags(s):
    count = lax.axis_size("col")
    place = lax.rem(lax.axis_index("col") + count - s, count)
    return place > 0, place < count - 1


def near_place():
    return jnp.where(lax.rem(lax.axis_index("col"), 2) == 1, 1, lax.axis_size("col") - 1)


def late_body(taps, bands, ext, cols, pixels, share, *refs):
    filters_ref, swapped_ref, passed_ref = refs[:3]
    mains, spills, images = refs[3:6], refs[6:9], refs[9:13]
    out_ref, tile_ref, *edge_refs, main_of, spill_of, y_ref = refs[13:]
    count, reach = 4, taps // 2
    middle = (lax.axis_index("col") == 1) | (lax.axis_index("col") == 2)
    tile_ref[...] = jnp.where(middle, swapped_ref[...], passed_ref[...])
    near = near_place()
    places = [0, 2, near]
    for s, main, spill in zip(places, mains, spills):
        main_of[s] = main[...]
        spill_of[s] = spill[...]
    main_of[count - near], spill_of[count - near] = tile_parts(filters_ref[...], tile_ref[...], y_ref, taps, bands, ext, cols)
    column = column_of(ext, cols)
    lane = lax.broadcasted_iota(jnp.int32, (1, 128), 1)
    for s in range(count):
        left, right = tile_flags(s)
        from_left = jnp.where((column < reach) & left, spill_of[(s + 1) % count], 0.0)
        from_right = jnp.where((column >= cols - reach) & right, spill_of[(s - 1) % count], 0.0)
        picture = images[s][...].astype(jnp.float32) * share
        pad = jnp.zeros((bands, ext - picture.shape[1]), jnp.float32)
        picture = roll(jnp.concatenate([picture, pad], axis=1), reach * cols)
        value = main_of[s] + from_left + from_right - picture
        out_ref[s] = value
        up = jnp.where(lane < 2 * reach * cols, value[:, :128], 0.0)
        down = value[:, pixels : pixels + 128]
        if len(edge_refs) == 1:
            edges = [jnp.where(lax.axis_index("row") == 0, down, up)]
        else:
            edges = [up, down]
        for ref, edge in zip(edge_refs, edges):
            ref[s] = edge


def join_body(count, pixels, turn, *refs):
    part_ref, *edge_refs, out_ref, send_ref = refs
    bands = part_ref.shape[1]

    def turned(x, step):
        step %= bands
        return x if step == 0 else jnp.concatenate([x[bands - step :], x[: bands - step]], axis=0)

    for s in range(count):
        pieces = [turned(ref[s], turn * sign) for ref, sign in zip(edge_refs, (-1, 1))]
        if len(pieces) == 1:
            first = lax.axis_index("row") == 0
            pieces = [jnp.where(first, pieces[0], 0.0), jnp.where(first, 0.0, pieces[0])]
        below, above = pieces
        own = part_ref[s]
        parts = [own[:, :128] + above, own[:, 128:pixels], own[:, pixels : pixels + 128] + below, own[:, pixels + 128 :]]
        value = jnp.concatenate([part for part in parts if part.shape[1]], axis=1)
        out_ref[s] = value
        send_ref[s] = value.astype(jnp.bfloat16)


def resid_body(ext, rows, cols, reach, peers, *refs):
    own_ref, others, out_ref = refs[0], refs[1 : 1 + peers], refs[1 + peers]
    line = lax.broadcasted_iota(jnp.int32, (1, ext), 1) // cols
    place, places = lax.axis_index("row"), lax.axis_size("row")
    real = ((line >= reach) | (place > 0)) & ((line < rows + reach) | (place < places - 1)) & (line < rows + 2 * reach)
    for s in range(out_ref.shape[0]):
        value = own_ref[s]
        for other in others:
            value = value + other[s].astype(jnp.float32)
        out_ref[s] = jnp.where(real, value, 0.0).astype(jnp.bfloat16).astype(jnp.float32)


def windows_of(taps, bands, ext, rows, cols, s, resid_ref, windows_ref):
    reach = taps // 2
    pixels = rows * cols
    count = resid_ref.shape[0]
    column = column_of(ext, cols)
    left, right = tile_flags(s)
    own = resid_ref[s]
    to_left = jnp.where(left, resid_ref[lax.rem(s + 1, count)], 0.0)
    to_right = jnp.where(right, resid_ref[lax.rem(s + count - 1, count)], 0.0)
    for b in range(taps):
        step = b - reach
        if step == 0:
            view = own
        elif step > 0:
            view = jnp.where(column >= step, roll(own, step), roll(to_left, step - cols))
        else:
            view = jnp.where(column < cols + step, roll(own, step), roll(to_right, step + cols))
        for a in range(taps):
            part = roll(view, -cols * (2 * reach - a))[:, :pixels]
            at = (a * taps + b) * bands
            windows_ref[at : at + bands, :] = part.astype(jnp.bfloat16)


def back_body(taps, bands, ext, rows, cols, which, peers, *refs):
    near = near_place()
    s = {"own": 0, "two": 2, "near": near, "far": 4 - near}[which]
    turned_ref = refs[0]
    if peers is None:
        resid_ref, (windows_ref, back_ref) = refs[1], refs[2:]
    else:
        windows_ref, back_ref, resid_ref = refs[-3:]
        resid_body(ext, rows, cols, taps // 2, peers, *refs[1:-3], resid_ref)
    windows_of(taps, bands, ext, rows, cols, s, resid_ref, windows_ref)
    back = jnp.dot(turned_ref[...], windows_ref[...], preferred_element_type=jnp.float32)
    back_ref[...] = back.astype(back_ref.dtype)


def merge_body(back_ref, passed_ref, out_ref):
    out_ref[...] = (back_ref[...] + passed_ref[...].astype(jnp.float32)).astype(jnp.bfloat16)


def grad_body(count, *refs):
    windows, tiles, grad_ref = refs[:count], refs[count : 2 * count], refs[2 * count]
    total = None
    for s in range(count):
        term = jnp.dot(windows[s][...], tiles[s][...], preferred_element_type=jnp.float32)
        total = term if total is None else total + term
    grad_ref[...] = total


def codes_body(*refs):
    codes_ref, back_ref = refs[:2]
    others, out_ref = refs[2:-1], refs[-1]
    back = back_ref[...]
    for other in others:
        back = back + other[...].astype(jnp.float32)
    moved = codes_ref[...].astype(jnp.float32) - 0.05 * back.T
    out_ref[...] = (moved - jnp.clip(moved, -0.02, 0.02)).astype(jnp.bfloat16)


def adam_update(master, moment, second, grad):
    new_moment = 0.9 * moment + 0.1 * grad
    new_second = 0.999 * second + 0.001 * grad * grad
    new_dictionary = master - 0.05 * (new_moment / first_fix) / (
        jnp.sqrt(new_second / second_fix) + 1e-08
    )
    return (new_dictionary, new_moment, new_second)


def iteration(codes, image, master, moment, second):
    rows, cols, atoms = codes.shape
    own_bands, taps = master.shape[0], master.shape[1]
    groups, count, peers = lax.axis_size("row"), lax.axis_size("col"), lax.axis_size("atom")
    bands = groups * own_bands
    reach = taps // 2
    pixels = rows * cols
    ext = -(-(rows + 2 * reach) * cols // 128) * 128
    row_at, col_at = lax.axis_index("row"), lax.axis_index("col")

    assert count == 4
    tile = codes.reshape(pixels, atoms)
    two = along(codes, TWO).reshape(pixels, atoms)
    near = along(codes, NEAR).reshape(pixels, atoms)

    own_filters = jnp.transpose(master, (1, 2, 0, 3)).reshape(taps * taps, own_bands, atoms).astype(jnp.bfloat16)
    filters = [own_filters]
    for s in range(1, groups):
        filters.append(shifted(own_filters, "row", s))
    filters = jnp.concatenate(filters, axis=1).reshape(taps * taps * bands, atoms)
    turned = filters.T

    picture = image.reshape(pixels, groups, count, own_bands).transpose(1, 2, 3, 0)
    picture = jnp.stack([lax.dynamic_index_in_dim(picture, (row_at + groups - s) % groups, 0, False) for s in range(groups)])
    pieces = [lax.dynamic_index_in_dim(picture, (col_at + s) % count, 1, False).reshape(bands, pixels) for s in range(count)]
    images = []
    for s in range(count):
        images.append(pieces[s] if s == 0 else shifted(pieces[s], "col", s))

    passed = along(two, [(2, 3), (1, 0)])
    swapped = along(tile, INNER)

    size = struct((bands, ext), jnp.float32)
    y_scratch = [pltpu.VMEM((taps * taps * bands, pixels), jnp.float32)]
    tile_flops = 2 * taps * taps * bands * pixels * atoms
    mains, spills = [], []
    for early in [tile, two, near]:
        body = functools.partial(early_body, taps, bands, ext, cols)
        main, spill = call(body, [size, size], [filters, early], tile_flops, y_scratch)
        mains.append(main)
        spills.append(spill)
    edge = struct((count, bands, 128), jnp.float32)
    part_shape = (count, bands, ext)
    part, far, *edges = call(
        functools.partial(late_body, taps, bands, ext, cols, pixels, 1.0 / peers),
        [struct(part_shape, jnp.float32), struct(tile.shape, tile.dtype)] + [edge] * (1 if groups == 2 else 2),
        [filters, swapped, passed, *mains, *spills, *images],
        tile_flops,
        [pltpu.VMEM(part_shape, jnp.float32)] * 2 + y_scratch,
    )
    if groups == 2:
        edges = [shifted(edges[0], "row", 1)]
    else:
        edges = [moved_on(edges[0], "row", -1), moved_on(edges[1], "row", 1)]
    part, send = call(
        functools.partial(join_body, count, pixels, own_bands),
        [struct(part_shape, jnp.float32), struct(part_shape, jnp.bfloat16)],
        [part, *edges],
    )
    if peers <= 4:
        others = []
        for m in range(peers - 1, 0, -1):
            others.append(lax.ppermute(send, "atom", [(i, i ^ m) for i in range(peers)]))
    else:
        others = [(lax.psum(send, "atom").astype(jnp.float32) - send.astype(jnp.float32)).astype(jnp.bfloat16)]

    def back_of(which, dtype, *args, peers=None):
        outs = [struct((taps * taps * bands, pixels), jnp.bfloat16), struct((atoms, pixels), dtype)]
        if peers is not None:
            outs.append(struct(part_shape, jnp.float32))
        body = functools.partial(back_body, taps, bands, ext, rows, cols, which, peers)
        return call(body, outs, [turned, *args], tile_flops)

    far_windows, far_back, resid = back_of("far", jnp.bfloat16, part, *others, peers=len(others))
    home_pass = along(far_back, [(3, 2), (0, 1)])
    home_swap = along(far_back, INNER)
    near_windows, near_back = back_of("near", jnp.bfloat16, resid)
    home_near = along(near_back, NEAR)
    two_windows, two_back = back_of("two", jnp.float32, resid)
    own_windows, own_back = back_of("own", jnp.float32, resid)
    (two_back,) = call(merge_body, [struct((atoms, pixels), jnp.bfloat16)], [two_back, home_pass])
    home_two = along(two_back, TWO)
    (grad,) = call(
        functools.partial(grad_body, count),
        [struct((taps * taps * bands, atoms), jnp.float32)],
        [own_windows, two_windows, near_windows, far_windows, tile, two, near, far],
        tile_flops * count,
    )
    grad = grad.reshape(taps * taps, groups, own_bands, atoms)
    own_grad = grad[:, 0]
    for s in range(1, groups):
        piece = grad[:, s].astype(jnp.bfloat16)
        piece = shifted(piece, "row", -s)
        own_grad = own_grad + piece.astype(jnp.float32)
    own_grad = jnp.transpose(own_grad.reshape(taps, taps, own_bands, atoms), (2, 0, 1, 3))
    new_dictionary, new_moment, new_second = adam_update(master, moment, second, own_grad)
    (new_codes,) = call(
        codes_body, [struct((pixels, atoms), jnp.bfloat16)], [tile, own_back, home_near, home_swap, home_two]
    )
    return (new_codes.reshape(rows, cols, atoms), new_dictionary, new_moment, new_second)


def solution(mesh):
    return jax.shard_map(
        iteration,
        mesh=mesh,
        in_specs=(
            P("row", "col", "atom"),
            P("row", "col", None),
            P(("row", "col"), None, None, "atom"),
            P(("row", "col"), None, None, "atom"),
            P(("row", "col"), None, None, "atom"),
        ),
        out_specs=(
            P("row", "col", "atom"),
            P(("row", "col"), None, None, "atom"),
            P(("row", "col"), None, None, "atom"),
            P(("row", "col"), None, None, "atom"),
        ),
        check_vma=False,
    )
```

```python
import functools

import jax
import jax.numpy as jnp
from jax import lax
from jax.experimental import pallas as pl
from jax.experimental.pallas import tpu as pltpu
from jax.sharding import PartitionSpec as P


first_fix = 0.9999734386011124
second_fix = 0.09520785288629038


def shifted(x, axis, step):
    count = lax.axis_size(axis)
    return lax.ppermute(x, axis, [(i, (i + step) % count) for i in range(count)])


def moved_on(x, axis, step):
    count = lax.axis_size(axis)
    return lax.ppermute(x, axis, [(i, i + step) for i in range(count) if 0 <= i + step < count])


def call(body, outs, args, flops=0, scratch=()):
    moved = sum(a.size * a.dtype.itemsize for a in args) + sum(o.size * o.dtype.itemsize for o in outs)
    return pl.pallas_call(
        body,
        out_shape=outs,
        in_specs=[pl.BlockSpec(memory_space=pltpu.VMEM)] * len(args),
        out_specs=[pl.BlockSpec(memory_space=pltpu.VMEM)] * len(outs),
        scratch_shapes=list(scratch),
        cost_estimate=pl.CostEstimate(flops=flops, bytes_accessed=moved, transcendentals=0),
        compiler_params=pltpu.CompilerParams(vmem_limit_bytes=24 << 20),
    )(*args)


def roll(x, amount):
    amount %= x.shape[1]
    return pltpu.roll(x, amount, 1) if amount else x


def struct(shape, dtype):
    return jax.ShapeDtypeStruct(shape, dtype)


def column_of(ext, cols):
    return lax.broadcasted_iota(jnp.int32, (1, ext), 1) % cols


def tile_parts(filters, tile, y_ref, taps, bands, ext, cols):
    reach = taps // 2
    y_ref[...] = lax.dot_general(filters, tile, (((1,), (1,)), ((), ())), preferred_element_type=jnp.float32)
    pixels = tile.shape[0]
    column = column_of(ext, cols)
    main = jnp.zeros((bands, ext), jnp.float32)
    to_right = jnp.zeros((bands, ext), jnp.float32)
    to_left = jnp.zeros((bands, ext), jnp.float32)
    tail = jnp.zeros((bands, ext - pixels), jnp.float32)
    for b in range(taps):
        total = None
        for a in range(taps):
            term = jnp.concatenate([y_ref[pl.ds((a * taps + b) * bands, bands), :], tail], axis=1)
            total = term if total is None else roll(total, cols) + term
        step = reach - b
        turned = roll(total, step)
        if step > 0:
            inside = column >= step
            to_right = to_right + jnp.where(inside, 0.0, turned)
        elif step < 0:
            inside = column < cols + step
            to_left = to_left + jnp.where(inside, 0.0, turned)
        main = main + (turned if step == 0 else jnp.where(inside, turned, 0.0))
    return main, roll(to_right, -cols) + roll(to_left, cols)


def early_body(taps, bands, ext, cols, filters_ref, tile_ref, main_ref, spill_ref, y_ref):
    main, spill = tile_parts(filters_ref[...], tile_ref[...], y_ref, taps, bands, ext, cols)
    main_ref[...] = main
    spill_ref[...] = spill


def tile_flags(s):
    count = lax.axis_size("col")
    place = lax.rem(lax.axis_index("col") + count - s, count)
    return place > 0, place < count - 1


def edges_of(value, pixels, reach, cols, places):
    lane = lax.broadcasted_iota(jnp.int32, (1, 128), 1)
    up = jnp.where(lane < 2 * reach * cols, value[:, :128], 0.0)
    down = value[:, pixels : pixels + 128]
    return [jnp.where(lax.axis_index("row") == 0, down, up)] if places == 1 else [up, down]


def sum_body(taps, bands, ext, cols, pixels, share, order, *refs):
    known, count = len(order), 4
    main_of = dict(zip(order, refs[:known]))
    spill_of = dict(zip(order, refs[known : 2 * known]))
    images = refs[2 * known : 2 * known + count]
    out_ref, *edge_refs = refs[2 * known + count :]
    reach = taps // 2
    column = column_of(ext, cols)
    for s in range(count):
        left, right = tile_flags(s)
        picture = images[s][...].astype(jnp.float32) * -share
        pad = jnp.zeros((bands, ext - pixels), jnp.float32)
        value = roll(jnp.concatenate([picture, pad], axis=1), reach * cols)
        if s in order:
            value = value + main_of[s][...]
        if (s + 1) % count in order:
            value = value + jnp.where((column < reach) & left, spill_of[(s + 1) % count][...], 0.0)
        if (s - 1) % count in order:
            value = value + jnp.where((column >= cols - reach) & right, spill_of[(s - 1) % count][...], 0.0)
        out_ref[s] = value
        for ref, edge in zip(edge_refs, edges_of(value, pixels, reach, cols, len(edge_refs))):
            ref[s] = edge


def late_body(taps, bands, ext, cols, pixels, filters_ref, tile_ref, out_ref, *refs):
    *edge_refs, y_ref = refs
    values = tile_parts(filters_ref[...], tile_ref[...], y_ref, taps, bands, ext, cols)
    for at, value in enumerate(values):
        out_ref[at] = value
        for ref, edge in zip(edge_refs, edges_of(value, pixels, taps // 2, cols, len(edge_refs))):
            ref[at] = edge


def join_body(pixels, turn, edges, *refs):
    part_ref, edge_refs, out_ref, send_refs = refs[0], refs[1 : 1 + edges], refs[1 + edges], refs[2 + edges :]
    count, bands = part_ref.shape[:2]

    def turned(x, step):
        step %= bands
        return x if step == 0 else jnp.concatenate([x[bands - step :], x[: bands - step]], axis=0)

    for s in range(count):
        pieces = [turned(ref[s], turn * sign) for ref, sign in zip(edge_refs, (-1, 1))]
        if len(pieces) == 1:
            first = lax.axis_index("row") == 0
            pieces = [jnp.where(first, pieces[0], 0.0), jnp.where(first, 0.0, pieces[0])]
        below, above = pieces
        own = part_ref[s]
        parts = [own[:, :128] + above, own[:, 128:pixels], own[:, pixels : pixels + 128] + below, own[:, pixels + 128 :]]
        value = jnp.concatenate([part for part in parts if part.shape[1]], axis=1)
        out_ref[s] = value
        for send_ref in send_refs:
            send_ref[s] = value.astype(jnp.bfloat16)


def real_lines(ext, rows, cols, reach):
    line = lax.broadcasted_iota(jnp.int32, (1, ext), 1) // cols
    place, places = lax.axis_index("row"), lax.axis_size("row")
    return ((line >= reach) | (place > 0)) & ((line < rows + reach) | (place < places - 1)) & (line < rows + 2 * reach)


def added(s, refs):
    value = refs[0][s]
    for ref in refs[1:]:
        value = value + ref[s].astype(jnp.float32)
    return value


def rounded(real, value):
    return jnp.where(real, value, 0.0).astype(jnp.bfloat16).astype(jnp.float32)


def windows_of(taps, bands, ext, rows, cols, s, resid_ref, windows_ref):
    reach = taps // 2
    pixels = rows * cols
    count = resid_ref.shape[0]
    column = column_of(ext, cols)
    left, right = tile_flags(s)
    own = resid_ref[s]
    to_left = jnp.where(left, resid_ref[lax.rem(s + 1, count)], 0.0)
    to_right = jnp.where(right, resid_ref[lax.rem(s + count - 1, count)], 0.0)
    for b in range(taps):
        step = b - reach
        if step == 0:
            view = own
        elif step > 0:
            view = jnp.where(column >= step, roll(own, step), roll(to_left, step - cols))
        else:
            view = jnp.where(column < cols + step, roll(own, step), roll(to_right, step + cols))
        for a in range(taps):
            part = roll(view, -cols * (2 * reach - a))[:, :pixels]
            at = (a * taps + b) * bands
            windows_ref[at : at + bands, :] = part.astype(jnp.bfloat16)


def back_of(taps, bands, ext, rows, cols, s, turned_ref, resid_ref, windows_ref, back_ref):
    windows_of(taps, bands, ext, rows, cols, s, resid_ref, windows_ref)
    back = jnp.dot(turned_ref[...], windows_ref[...], preferred_element_type=jnp.float32)
    back_ref[...] = back.astype(back_ref.dtype)


def first_back_body(taps, bands, ext, rows, cols, s, turned_ref, *refs):
    *terms, windows_ref, back_ref, sum_ref, resid_ref = refs
    real = real_lines(ext, rows, cols, taps // 2)
    for tile in range(sum_ref.shape[0]):
        value = added(tile, terms)
        sum_ref[tile] = value
        resid_ref[tile] = rounded(real, value)
    back_of(taps, bands, ext, rows, cols, s, turned_ref, resid_ref, windows_ref, back_ref)


def second_back_body(taps, bands, ext, rows, cols, s, late, turned_ref, sum_ref, *refs):
    *terms, windows_ref, back_ref, resid_ref = refs
    count, reach = sum_ref.shape[0], taps // 2
    real = real_lines(ext, rows, cols, reach)
    column = column_of(ext, cols)
    main, spill = added(0, terms), added(1, terms)
    for tile in range(count):
        value = sum_ref[tile]
        left, right = tile_flags(tile)
        if tile == late:
            value = value + main
        if (tile + 1) % count == late:
            value = value + jnp.where((column < reach) & left, spill, 0.0)
        if (tile - 1) % count == late:
            value = value + jnp.where((column >= cols - reach) & right, spill, 0.0)
        resid_ref[tile] = rounded(real, value)
    back_of(taps, bands, ext, rows, cols, s, turned_ref, resid_ref, windows_ref, back_ref)


def turn_body(filters_ref, out_ref):
    out_ref[...] = filters_ref[...].T


def grad_body(count, *refs):
    windows, tiles, grad_ref = refs[:count], refs[count : 2 * count], refs[2 * count]
    total = None
    for s in range(count):
        term = jnp.dot(windows[s][...], tiles[s][...], preferred_element_type=jnp.float32)
        total = term if total is None else total + term
    grad_ref[...] = total


def codes_body(*refs):
    codes_ref, back_ref = refs[:2]
    others, out_ref = refs[2:-1], refs[-1]
    back = back_ref[...]
    for other in others:
        back = back + other[...].astype(jnp.float32)
    moved = codes_ref[...].astype(jnp.float32) - 0.05 * back.T
    out_ref[...] = (moved - jnp.clip(moved, -0.02, 0.02)).astype(jnp.bfloat16)


def adam_update(master, moment, second, grad):
    new_moment = 0.9 * moment + 0.1 * grad
    new_second = 0.999 * second + 0.001 * grad * grad
    new_dictionary = master - 0.05 * (new_moment / first_fix) / (
        jnp.sqrt(new_second / second_fix) + 1e-08
    )
    return (new_dictionary, new_moment, new_second)


def iteration(codes, image, master, moment, second):
    rows, cols, atoms = codes.shape
    own_bands, taps = master.shape[0], master.shape[1]
    groups, count, peers = lax.axis_size("row"), lax.axis_size("col"), lax.axis_size("atom")
    bands = groups * own_bands
    reach = taps // 2
    pixels = rows * cols
    ext = -(-(rows + 2 * reach) * cols // 128) * 128
    row_at, col_at = lax.axis_index("row"), lax.axis_index("col")

    assert count == 4
    tiles = {0: codes.reshape(pixels, atoms)}
    for s in (2, 3, 1):
        tiles[s] = shifted(codes, "col", s).reshape(pixels, atoms)

    own_filters = jnp.transpose(master, (1, 2, 0, 3)).reshape(taps * taps, own_bands, atoms).astype(jnp.bfloat16)
    filters = [own_filters]
    for s in range(1, groups):
        filters.append(shifted(own_filters, "row", s))
    filters = jnp.concatenate(filters, axis=1).reshape(taps * taps * bands, atoms)
    (turned,) = call(turn_body, [struct(filters.shape[::-1], filters.dtype)], [filters])

    picture = image.reshape(pixels, groups, count, own_bands).transpose(1, 2, 3, 0)
    picture = jnp.stack([lax.dynamic_index_in_dim(picture, (row_at + groups - s) % groups, 0, False) for s in range(groups)])
    pieces = [lax.dynamic_index_in_dim(picture, (col_at + s) % count, 1, False).reshape(bands, pixels) for s in range(count)]
    images = []
    for s in range(count):
        images.append(pieces[s] if s == 0 else shifted(pieces[s], "col", s))

    size = struct((bands, ext), jnp.float32)
    y_scratch = [pltpu.VMEM((taps * taps * bands, pixels), jnp.float32)]
    tile_flops = 2 * taps * taps * bands * pixels * atoms
    edges_out = 1 if groups == 2 else 2

    def whole_rows(part, edges):
        if groups == 2:
            edges = [shifted(edges[0], "row", 1)]
        else:
            edges = [moved_on(edges[0], "row", -1), moved_on(edges[1], "row", 1)]
        return call(
            functools.partial(join_body, pixels, own_bands, edges_out),
            [struct(part.shape, jnp.float32)] + [struct(part.shape, jnp.bfloat16)] * copies,
            [part, *edges],
        )

    copies = peers - 1 if peers <= 4 else 1

    def all_atoms(part, *sends):
        if peers > 4:
            (send,) = sends
            return [part, (lax.psum(send, "atom").astype(jnp.float32) - send.astype(jnp.float32)).astype(jnp.bfloat16)]
        terms = [part]
        for m in range(peers - 1, 0, -1):
            terms.append(lax.ppermute(sends[m - 1], "atom", [(i, i ^ m) for i in range(peers)]))
        return terms

    early = (0, 2, 3)
    mains, spills = [], []
    for s in early:
        body = functools.partial(early_body, taps, bands, ext, cols)
        main, spill = call(body, [size, size], [filters, tiles[s]], tile_flops, y_scratch)
        mains.append(main)
        spills.append(spill)
    part, *edges = call(
        functools.partial(sum_body, taps, bands, ext, cols, pixels, 1.0 / peers, early),
        [struct((count, bands, ext), jnp.float32)] + [struct((count, bands, 128), jnp.float32)] * edges_out,
        [*mains, *spills, *images],
    )
    terms = all_atoms(*whole_rows(part, edges))

    part, *edges = call(
        functools.partial(late_body, taps, bands, ext, cols, pixels),
        [struct((2, bands, ext), jnp.float32)] + [struct((2, bands, 128), jnp.float32)] * edges_out,
        [filters, tiles[1]],
        tile_flops,
        y_scratch,
    )
    late_terms = all_atoms(*whole_rows(part, edges))

    shape = (taps, bands, ext, rows, cols)
    resid = struct((count, bands, ext), jnp.float32)
    windows, backs, received = {}, {}, []
    for s in (3, 2, 1, 0):
        outs = [struct((taps * taps * bands, pixels), jnp.bfloat16), struct((atoms, pixels), jnp.bfloat16 if s else jnp.float32)]
        if s == 3:
            body = functools.partial(first_back_body, *shape, s)
            windows[s], backs[s], total, _ = call(body, outs + [resid] * 2, [turned, *terms], tile_flops)
        elif s == 2:
            body = functools.partial(second_back_body, *shape, s, 1)
            args = [turned, total, *late_terms]
            windows[s], backs[s], resid = call(body, outs + [resid], args, tile_flops)
        else:
            body = functools.partial(back_of, *shape, s)
            windows[s], backs[s] = call(body, outs, [turned, resid], tile_flops)
        if s:
            received.append(shifted(backs[s], "col", -s))
    (grad,) = call(
        functools.partial(grad_body, count),
        [struct((taps * taps * bands, atoms), jnp.float32)],
        [windows[s] for s in range(count)] + [tiles[s] for s in range(count)],
        tile_flops * count,
    )
    grad = grad.reshape(taps * taps, groups, own_bands, atoms)
    own_grad = grad[:, 0]
    for s in range(1, groups):
        piece = grad[:, s].astype(jnp.bfloat16)
        piece = shifted(piece, "row", -s)
        own_grad = own_grad + piece.astype(jnp.float32)
    own_grad = jnp.transpose(own_grad.reshape(taps, taps, own_bands, atoms), (2, 0, 1, 3))
    new_dictionary, new_moment, new_second = adam_update(master, moment, second, own_grad)
    (new_codes,) = call(codes_body, [struct((pixels, atoms), jnp.bfloat16)], [tiles[0], backs[0], *received])
    return (new_codes.reshape(rows, cols, atoms), new_dictionary, new_moment, new_second)


def solution(mesh):
    return jax.shard_map(
        iteration,
        mesh=mesh,
        in_specs=(
            P("row", "col", "atom"),
            P("row", "col", None),
            P(("row", "col"), None, None, "atom"),
            P(("row", "col"), None, None, "atom"),
            P(("row", "col"), None, None, "atom"),
        ),
        out_specs=(
            P("row", "col", "atom"),
            P(("row", "col"), None, None, "atom"),
            P(("row", "col"), None, None, "atom"),
            P(("row", "col"), None, None, "atom"),
        ),
        check_vma=False,
    )
```

```python
import functools

import jax
import jax.numpy as jnp
from jax import lax
from jax.experimental import pallas as pl
from jax.experimental.pallas import tpu as pltpu
from jax.sharding import PartitionSpec as P


first_fix = 0.9999734386011124
second_fix = 0.09520785288629038


def shifted(x, axis, step):
    count = lax.axis_size(axis)
    return lax.ppermute(x, axis, [(i, (i + step) % count) for i in range(count)])


def moved_on(x, axis, step):
    count = lax.axis_size(axis)
    return lax.ppermute(x, axis, [(i, i + step) for i in range(count) if 0 <= i + step < count])


TWO = [(0, 2), (1, 3), (2, 0), (3, 1)]
NEAR = [(0, 1), (1, 0), (2, 3), (3, 2)]
INNER = [(1, 2), (2, 1)]


def along(x, pairs):
    return lax.ppermute(x, "col", pairs)


def call(body, outs, args, flops=0, scratch=()):
    moved = sum(a.size * a.dtype.itemsize for a in args) + sum(o.size * o.dtype.itemsize for o in outs)
    return pl.pallas_call(
        body,
        out_shape=outs,
        in_specs=[pl.BlockSpec(memory_space=pltpu.VMEM)] * len(args),
        out_specs=[pl.BlockSpec(memory_space=pltpu.VMEM)] * len(outs),
        scratch_shapes=list(scratch),
        cost_estimate=pl.CostEstimate(flops=flops, bytes_accessed=moved, transcendentals=0),
        compiler_params=pltpu.CompilerParams(vmem_limit_bytes=24 << 20),
    )(*args)


def roll(x, amount):
    amount %= x.shape[1]
    return pltpu.roll(x, amount, 1) if amount else x


def struct(shape, dtype):
    return jax.ShapeDtypeStruct(shape, dtype)


def column_of(ext, cols):
    return lax.broadcasted_iota(jnp.int32, (1, ext), 1) % cols


def tile_parts(filters, tile, y_ref, taps, bands, ext, cols):
    reach = taps // 2
    y_ref[...] = lax.dot_general(filters, tile, (((1,), (1,)), ((), ())), preferred_element_type=jnp.float32)
    pixels = tile.shape[0]
    column = column_of(ext, cols)
    main = jnp.zeros((bands, ext), jnp.float32)
    to_right = jnp.zeros((bands, ext), jnp.float32)
    to_left = jnp.zeros((bands, ext), jnp.float32)
    tail = jnp.zeros((bands, ext - pixels), jnp.float32)
    for b in range(taps):
        total = None
        for a in range(taps):
            term = jnp.concatenate([y_ref[pl.ds((a * taps + b) * bands, bands), :], tail], axis=1)
            total = term if total is None else roll(total, cols) + term
        step = reach - b
        turned = roll(total, step)
        if step > 0:
            inside = column >= step
            to_right = to_right + jnp.where(inside, 0.0, turned)
        elif step < 0:
            inside = column < cols + step
            to_left = to_left + jnp.where(inside, 0.0, turned)
        main = main + (turned if step == 0 else jnp.where(inside, turned, 0.0))
    return main, roll(to_right, -cols) + roll(to_left, cols)


def early_body(taps, bands, ext, cols, filters_ref, tile_ref, main_ref, spill_ref, y_ref):
    main, spill = tile_parts(filters_ref[...], tile_ref[...], y_ref, taps, bands, ext, cols)
    main_ref[...] = main
    spill_ref[...] = spill


def tile_flags(s):
    count = lax.axis_size("col")
    place = lax.rem(lax.axis_index("col") + count - s, count)
    return place > 0, place < count - 1


def near_place():
    return jnp.where(lax.rem(lax.axis_index("col"), 2) == 1, 1, lax.axis_size("col") - 1)


def late_body(taps, bands, ext, cols, pixels, share, *refs):
    filters_ref, swapped_ref, passed_ref = refs[:3]
    mains, spills, images = refs[3:6], refs[6:9], refs[9:13]
    out_ref, tile_ref, *edge_refs, main_of, spill_of, y_ref = refs[13:]
    count, reach = 4, taps // 2
    middle = (lax.axis_index("col") == 1) | (lax.axis_index("col") == 2)
    tile_ref[...] = jnp.where(middle, swapped_ref[...], passed_ref[...])
    near = near_place()
    places = [0, 2, near]
    for s, main, spill in zip(places, mains, spills):
        main_of[s] = main[...]
        spill_of[s] = spill[...]
    main_of[count - near], spill_of[count - near] = tile_parts(filters_ref[...], tile_ref[...], y_ref, taps, bands, ext, cols)
    column = column_of(ext, cols)
    lane = lax.broadcasted_iota(jnp.int32, (1, 128), 1)
    for s in range(count):
        left, right = tile_flags(s)
        from_left = jnp.where((column < reach) & left, spill_of[(s + 1) % count], 0.0)
        from_right = jnp.where((column >= cols - reach) & right, spill_of[(s - 1) % count], 0.0)
        picture = images[s][...].astype(jnp.float32) * share
        pad = jnp.zeros((bands, ext - picture.shape[1]), jnp.float32)
        picture = roll(jnp.concatenate([picture, pad], axis=1), reach * cols)
        value = main_of[s] + from_left + from_right - picture
        out_ref[s] = value
        up = jnp.where(lane < 2 * reach * cols, value[:, :128], 0.0)
        down = value[:, pixels : pixels + 128]
        if len(edge_refs) == 1:
            edges = [jnp.where(lax.axis_index("row") == 0, down, up)]
        else:
            edges = [up, down]
        for ref, edge in zip(edge_refs, edges):
            ref[s] = edge


def join_body(count, pixels, turn, *refs):
    part_ref, *edge_refs, out_ref, send_ref = refs
    bands = part_ref.shape[1]

    def turned(x, step):
        step %= bands
        return x if step == 0 else jnp.concatenate([x[bands - step :], x[: bands - step]], axis=0)

    for s in range(count):
        pieces = [turned(ref[s], turn * sign) for ref, sign in zip(edge_refs, (-1, 1))]
        if len(pieces) == 1:
            first = lax.axis_index("row") == 0
            pieces = [jnp.where(first, pieces[0], 0.0), jnp.where(first, 0.0, pieces[0])]
        below, above = pieces
        own = part_ref[s]
        parts = [own[:, :128] + above, own[:, 128:pixels], own[:, pixels : pixels + 128] + below, own[:, pixels + 128 :]]
        value = jnp.concatenate([part for part in parts if part.shape[1]], axis=1)
        out_ref[s] = value
        send_ref[s] = value.astype(jnp.bfloat16)


def resid_body(ext, rows, cols, reach, peers, *refs):
    own_ref, others, out_ref = refs[0], refs[1 : 1 + peers], refs[1 + peers]
    line = lax.broadcasted_iota(jnp.int32, (1, ext), 1) // cols
    place, places = lax.axis_index("row"), lax.axis_size("row")
    real = ((line >= reach) | (place > 0)) & ((line < rows + reach) | (place < places - 1)) & (line < rows + 2 * reach)
    for s in range(out_ref.shape[0]):
        value = own_ref[s]
        for other in others:
            value = value + other[s].astype(jnp.float32)
        out_ref[s] = jnp.where(real, value, 0.0).astype(jnp.bfloat16).astype(jnp.float32)


def windows_of(taps, bands, ext, rows, cols, s, resid_ref, windows_ref):
    reach = taps // 2
    pixels = rows * cols
    count = resid_ref.shape[0]
    column = column_of(ext, cols)
    left, right = tile_flags(s)
    own = resid_ref[s]
    to_left = jnp.where(left, resid_ref[lax.rem(s + 1, count)], 0.0)
    to_right = jnp.where(right, resid_ref[lax.rem(s + count - 1, count)], 0.0)
    for b in range(taps):
        step = b - reach
        if step == 0:
            view = own
        elif step > 0:
            view = jnp.where(column >= step, roll(own, step), roll(to_left, step - cols))
        else:
            view = jnp.where(column < cols + step, roll(own, step), roll(to_right, step + cols))
        for a in range(taps):
            part = roll(view, -cols * (2 * reach - a))[:, :pixels]
            at = (a * taps + b) * bands
            windows_ref[at : at + bands, :] = part.astype(jnp.bfloat16)


def back_body(taps, bands, ext, rows, cols, which, peers, *refs):
    near = near_place()
    s = {"own": 0, "two": 2, "near": near, "far": 4 - near}[which]
    turned_ref = refs[0]
    if peers is None:
        resid_ref, (windows_ref, *back_refs) = refs[1], refs[2:]
    else:
        windows_ref, *back_refs, resid_ref = refs[-3:]
        resid_body(ext, rows, cols, taps // 2, peers, *refs[1:-3], resid_ref)
    windows_of(taps, bands, ext, rows, cols, s, resid_ref, windows_ref)
    back = jnp.dot(turned_ref[...], windows_ref[...], preferred_element_type=jnp.float32)
    for back_ref in back_refs:
        back_ref[...] = back.astype(back_ref.dtype)


def merge_body(back_ref, passed_ref, out_ref):
    out_ref[...] = (back_ref[...] + passed_ref[...].astype(jnp.float32)).astype(jnp.bfloat16)


def turn_body(filters_ref, out_ref):
    out_ref[...] = filters_ref[...].T


def grad_body(count, *refs):
    windows, tiles, grad_ref = refs[:count], refs[count : 2 * count], refs[2 * count]
    total = None
    for s in range(count):
        term = jnp.dot(windows[s][...], tiles[s][...], preferred_element_type=jnp.float32)
        total = term if total is None else total + term
    grad_ref[...] = total


def codes_body(*refs):
    codes_ref, back_ref = refs[:2]
    others, out_ref = refs[2:-1], refs[-1]
    back = back_ref[...]
    for other in others:
        back = back + other[...].astype(jnp.float32)
    moved = codes_ref[...].astype(jnp.float32) - 0.05 * back.T
    out_ref[...] = (moved - jnp.clip(moved, -0.02, 0.02)).astype(jnp.bfloat16)


def adam_update(master, moment, second, grad):
    new_moment = 0.9 * moment + 0.1 * grad
    new_second = 0.999 * second + 0.001 * grad * grad
    new_dictionary = master - 0.05 * (new_moment / first_fix) / (
        jnp.sqrt(new_second / second_fix) + 1e-08
    )
    return (new_dictionary, new_moment, new_second)


def iteration(codes, image, master, moment, second):
    rows, cols, atoms = codes.shape
    own_bands, taps = master.shape[0], master.shape[1]
    groups, count, peers = lax.axis_size("row"), lax.axis_size("col"), lax.axis_size("atom")
    bands = groups * own_bands
    reach = taps // 2
    pixels = rows * cols
    ext = -(-(rows + 2 * reach) * cols // 128) * 128
    row_at, col_at = lax.axis_index("row"), lax.axis_index("col")

    assert count == 4
    tile = codes.reshape(pixels, atoms)
    two = along(codes, TWO).reshape(pixels, atoms)
    near = along(codes, NEAR).reshape(pixels, atoms)
    swapped = along(codes, INNER).reshape(pixels, atoms)

    own_filters = jnp.transpose(master, (1, 2, 0, 3)).reshape(taps * taps, own_bands, atoms).astype(jnp.bfloat16)
    filters = [own_filters]
    for s in range(1, groups):
        filters.append(shifted(own_filters, "row", s))
    filters = jnp.concatenate(filters, axis=1).reshape(taps * taps * bands, atoms)
    (turned,) = call(turn_body, [struct(filters.shape[::-1], filters.dtype)], [filters])

    picture = image.reshape(pixels, groups, count, own_bands).transpose(1, 2, 3, 0)
    picture = jnp.stack([lax.dynamic_index_in_dim(picture, (row_at + groups - s) % groups, 0, False) for s in range(groups)])
    pieces = [lax.dynamic_index_in_dim(picture, (col_at + s) % count, 1, False).reshape(bands, pixels) for s in range(count)]
    images = []
    for s in range(count):
        images.append(pieces[s] if s == 0 else shifted(pieces[s], "col", s))

    passed = along(two, [(2, 3), (1, 0)])

    size = struct((bands, ext), jnp.float32)
    y_scratch = [pltpu.VMEM((taps * taps * bands, pixels), jnp.float32)]
    tile_flops = 2 * taps * taps * bands * pixels * atoms
    mains, spills = [], []
    for early in [tile, two, near]:
        body = functools.partial(early_body, taps, bands, ext, cols)
        main, spill = call(body, [size, size], [filters, early], tile_flops, y_scratch)
        mains.append(main)
        spills.append(spill)
    edge = struct((count, bands, 128), jnp.float32)
    part_shape = (count, bands, ext)
    part, far, *edges = call(
        functools.partial(late_body, taps, bands, ext, cols, pixels, 1.0 / peers),
        [struct(part_shape, jnp.float32), struct(tile.shape, tile.dtype)] + [edge] * (1 if groups == 2 else 2),
        [filters, swapped, passed, *mains, *spills, *images],
        tile_flops,
        [pltpu.VMEM(part_shape, jnp.float32)] * 2 + y_scratch,
    )
    if groups == 2:
        edges = [shifted(edges[0], "row", 1)]
    else:
        edges = [moved_on(edges[0], "row", -1), moved_on(edges[1], "row", 1)]
    part, send = call(
        functools.partial(join_body, count, pixels, own_bands),
        [struct(part_shape, jnp.float32), struct(part_shape, jnp.bfloat16)],
        [part, *edges],
    )
    if peers <= 4:
        others = []
        for m in range(peers - 1, 0, -1):
            others.append(lax.ppermute(send, "atom", [(i, i ^ m) for i in range(peers)]))
    else:
        others = [(lax.psum(send, "atom").astype(jnp.float32) - send.astype(jnp.float32)).astype(jnp.bfloat16)]

    def back_of(which, dtypes, *args, peers=None):
        outs = [struct((taps * taps * bands, pixels), jnp.bfloat16)] + [struct((atoms, pixels), dtype) for dtype in dtypes]
        if peers is not None:
            outs.append(struct(part_shape, jnp.float32))
        body = functools.partial(back_body, taps, bands, ext, rows, cols, which, peers)
        return call(body, outs, [turned, *args], tile_flops)

    far_windows, far_back, resid = back_of("far", [jnp.bfloat16], part, *others, peers=len(others))
    home_pass = along(far_back, [(3, 2), (0, 1)])
    home_swap = along(far_back, INNER)
    two_windows, two_back, two_send = back_of("two", [jnp.float32, jnp.bfloat16], resid)
    home_two = along(two_send, TWO[::3])
    near_windows, near_back = back_of("near", [jnp.bfloat16], resid)
    home_near = along(near_back, NEAR)
    own_windows, own_back = back_of("own", [jnp.float32], resid)
    (two_back,) = call(merge_body, [struct((atoms, pixels), jnp.bfloat16)], [two_back, home_pass])
    home_both = along(two_back, TWO[1:3])
    (grad,) = call(
        functools.partial(grad_body, count),
        [struct((taps * taps * bands, atoms), jnp.float32)],
        [own_windows, two_windows, near_windows, far_windows, tile, two, near, far],
        tile_flops * count,
    )
    grad = grad.reshape(taps * taps, groups, own_bands, atoms)
    own_grad = grad[:, 0]
    for s in range(1, groups):
        piece = grad[:, s].astype(jnp.bfloat16)
        piece = shifted(piece, "row", -s)
        own_grad = own_grad + piece.astype(jnp.float32)
    own_grad = jnp.transpose(own_grad.reshape(taps, taps, own_bands, atoms), (2, 0, 1, 3))
    new_dictionary, new_moment, new_second = adam_update(master, moment, second, own_grad)
    (new_codes,) = call(
        codes_body, [struct((pixels, atoms), jnp.bfloat16)], [tile, own_back, home_near, home_swap, home_two, home_both]
    )
    return (new_codes.reshape(rows, cols, atoms), new_dictionary, new_moment, new_second)


def solution(mesh):
    return jax.shard_map(
        iteration,
        mesh=mesh,
        in_specs=(
            P("row", "col", "atom"),
            P("row", "col", None),
            P(("row", "col"), None, None, "atom"),
            P(("row", "col"), None, None, "atom"),
            P(("row", "col"), None, None, "atom"),
        ),
        out_specs=(
            P("row", "col", "atom"),
            P(("row", "col"), None, None, "atom"),
            P(("row", "col"), None, None, "atom"),
            P(("row", "col"), None, None, "atom"),
        ),
        check_vma=False,
    )
```

```python
import functools

import jax
import jax.numpy as jnp
from jax import lax
from jax.experimental import pallas as pl
from jax.experimental.pallas import tpu as pltpu
from jax.sharding import PartitionSpec as P


first_fix = 0.9999734386011124
second_fix = 0.09520785288629038


def shifted(x, axis, step):
    count = lax.axis_size(axis)
    return lax.ppermute(x, axis, [(i, (i + step) % count) for i in range(count)])


def moved_on(x, axis, step):
    count = lax.axis_size(axis)
    return lax.ppermute(x, axis, [(i, i + step) for i in range(count) if 0 <= i + step < count])


TWO = [(0, 2), (1, 3), (2, 0), (3, 1)]
NEAR = [(0, 1), (1, 0), (2, 3), (3, 2)]
INNER = [(1, 2), (2, 1)]


def along(x, pairs):
    return lax.ppermute(x, "col", pairs)


def call(body, outs, args, flops=0, scratch=()):
    moved = sum(a.size * a.dtype.itemsize for a in args) + sum(o.size * o.dtype.itemsize for o in outs)
    return pl.pallas_call(
        body,
        out_shape=outs,
        in_specs=[pl.BlockSpec(memory_space=pltpu.VMEM)] * len(args),
        out_specs=[pl.BlockSpec(memory_space=pltpu.VMEM)] * len(outs),
        scratch_shapes=list(scratch),
        cost_estimate=pl.CostEstimate(flops=flops, bytes_accessed=moved, transcendentals=0),
        compiler_params=pltpu.CompilerParams(vmem_limit_bytes=24 << 20),
    )(*args)


def roll(x, amount):
    amount %= x.shape[1]
    return pltpu.roll(x, amount, 1) if amount else x


def struct(shape, dtype):
    return jax.ShapeDtypeStruct(shape, dtype)


def column_of(ext, cols):
    return lax.broadcasted_iota(jnp.int32, (1, ext), 1) % cols


def tile_parts(filters, tile, y_ref, taps, bands, ext, cols):
    reach = taps // 2
    y_ref[...] = lax.dot_general(filters, tile, (((1,), (1,)), ((), ())), preferred_element_type=jnp.float32)
    pixels = tile.shape[0]
    column = column_of(ext, cols)
    main = jnp.zeros((bands, ext), jnp.float32)
    to_right = jnp.zeros((bands, ext), jnp.float32)
    to_left = jnp.zeros((bands, ext), jnp.float32)
    tail = jnp.zeros((bands, ext - pixels), jnp.float32)
    for b in range(taps):
        total = None
        for a in range(taps):
            term = jnp.concatenate([y_ref[pl.ds((a * taps + b) * bands, bands), :], tail], axis=1)
            total = term if total is None else roll(total, cols) + term
        step = reach - b
        turned = roll(total, step)
        if step > 0:
            inside = column >= step
            to_right = to_right + jnp.where(inside, 0.0, turned)
        elif step < 0:
            inside = column < cols + step
            to_left = to_left + jnp.where(inside, 0.0, turned)
        main = main + (turned if step == 0 else jnp.where(inside, turned, 0.0))
    return main, roll(to_right, -cols) + roll(to_left, cols)


def early_body(taps, bands, ext, cols, filters_ref, tile_ref, main_ref, spill_ref, y_ref):
    main, spill = tile_parts(filters_ref[...], tile_ref[...], y_ref, taps, bands, ext, cols)
    main_ref[...] = main
    spill_ref[...] = spill


def tile_flags(s):
    count = lax.axis_size("col")
    place = lax.rem(lax.axis_index("col") + count - s, count)
    return place > 0, place < count - 1


def near_place():
    return jnp.where(lax.rem(lax.axis_index("col"), 2) == 1, 1, lax.axis_size("col") - 1)


def late_body(taps, bands, ext, cols, pixels, share, *refs):
    filters_ref, swapped_ref, passed_ref = refs[:3]
    mains, spills, images = refs[3:6], refs[6:9], refs[9:13]
    out_ref, tile_ref, *edge_refs, main_of, spill_of, y_ref = refs[13:]
    count, reach = 4, taps // 2
    middle = (lax.axis_index("col") == 1) | (lax.axis_index("col") == 2)
    tile_ref[...] = jnp.where(middle, swapped_ref[...], passed_ref[...])
    near = near_place()
    places = [0, 2, near]
    for s, main, spill in zip(places, mains, spills):
        main_of[s] = main[...]
        spill_of[s] = spill[...]
    main_of[count - near], spill_of[count - near] = tile_parts(filters_ref[...], tile_ref[...], y_ref, taps, bands, ext, cols)
    column = column_of(ext, cols)
    lane = lax.broadcasted_iota(jnp.int32, (1, 128), 1)
    for s in range(count):
        left, right = tile_flags(s)
        from_left = jnp.where((column < reach) & left, spill_of[(s + 1) % count], 0.0)
        from_right = jnp.where((column >= cols - reach) & right, spill_of[(s - 1) % count], 0.0)
        picture = images[s][...].astype(jnp.float32) * share
        pad = jnp.zeros((bands, ext - picture.shape[1]), jnp.float32)
        picture = roll(jnp.concatenate([picture, pad], axis=1), reach * cols)
        value = main_of[s] + from_left + from_right - picture
        out_ref[s] = value
        up = jnp.where(lane < 2 * reach * cols, value[:, :128], 0.0)
        down = value[:, pixels : pixels + 128]
        if len(edge_refs) == 1:
            edges = [jnp.where(lax.axis_index("row") == 0, down, up)]
        else:
            edges = [up, down]
        for ref, edge in zip(edge_refs, edges):
            ref[s] = edge


def join_body(count, pixels, turn, *refs):
    part_ref, *edge_refs, out_ref, send_ref = refs
    bands = part_ref.shape[1]

    def turned(x, step):
        step %= bands
        return x if step == 0 else jnp.concatenate([x[bands - step :], x[: bands - step]], axis=0)

    for s in range(count):
        pieces = [turned(ref[s], turn * sign) for ref, sign in zip(edge_refs, (-1, 1))]
        if len(pieces) == 1:
            first = lax.axis_index("row") == 0
            pieces = [jnp.where(first, pieces[0], 0.0), jnp.where(first, 0.0, pieces[0])]
        below, above = pieces
        own = part_ref[s]
        parts = [own[:, :128] + above, own[:, 128:pixels], own[:, pixels : pixels + 128] + below, own[:, pixels + 128 :]]
        value = jnp.concatenate([part for part in parts if part.shape[1]], axis=1)
        out_ref[s] = value
        send_ref[s] = value.astype(jnp.bfloat16)


def resid_body(ext, rows, cols, reach, peers, *refs):
    own_ref, others, out_ref = refs[0], refs[1 : 1 + peers], refs[1 + peers]
    line = lax.broadcasted_iota(jnp.int32, (1, ext), 1) // cols
    place, places = lax.axis_index("row"), lax.axis_size("row")
    real = ((line >= reach) | (place > 0)) & ((line < rows + reach) | (place < places - 1)) & (line < rows + 2 * reach)
    for s in range(out_ref.shape[0]):
        value = own_ref[s]
        for other in others:
            value = value + other[s].astype(jnp.float32)
        out_ref[s] = jnp.where(real, value, 0.0).astype(jnp.bfloat16).astype(jnp.float32)


def windows_of(taps, bands, ext, rows, cols, s, resid_ref, windows_ref):
    reach = taps // 2
    pixels = rows * cols
    count = resid_ref.shape[0]
    column = column_of(ext, cols)
    left, right = tile_flags(s)
    own = resid_ref[s]
    to_left = jnp.where(left, resid_ref[lax.rem(s + 1, count)], 0.0)
    to_right = jnp.where(right, resid_ref[lax.rem(s + count - 1, count)], 0.0)
    for b in range(taps):
        step = b - reach
        if step == 0:
            view = own
        elif step > 0:
            view = jnp.where(column >= step, roll(own, step), roll(to_left, step - cols))
        else:
            view = jnp.where(column < cols + step, roll(own, step), roll(to_right, step + cols))
        for a in range(taps):
            part = roll(view, -cols * (2 * reach - a))[:, :pixels]
            at = (a * taps + b) * bands
            windows_ref[at : at + bands, :] = part.astype(jnp.bfloat16)


def back_body(taps, bands, ext, rows, cols, which, peers, *refs):
    near = near_place()
    s = {"own": 0, "two": 2, "near": near, "far": 4 - near}[which]
    turned_ref = refs[0]
    if peers is None:
        resid_ref, (windows_ref, *back_refs) = refs[1], refs[2:]
    else:
        windows_ref, *back_refs, resid_ref = refs[-3:]
        resid_body(ext, rows, cols, taps // 2, peers, *refs[1:-3], resid_ref)
    windows_of(taps, bands, ext, rows, cols, s, resid_ref, windows_ref)
    back = jnp.dot(turned_ref[...], windows_ref[...], preferred_element_type=jnp.float32)
    for back_ref in back_refs:
        back_ref[...] = back.astype(back_ref.dtype)


def merge_body(back_ref, passed_ref, out_ref):
    out_ref[...] = (back_ref[...] + passed_ref[...].astype(jnp.float32)).astype(jnp.bfloat16)


def turn_body(filters_ref, out_ref):
    out_ref[...] = filters_ref[...].T


def grad_body(count, *refs):
    windows, tiles, grad_ref = refs[:count], refs[count : 2 * count], refs[2 * count]
    total = None
    for s in range(count):
        term = jnp.dot(windows[s][...], tiles[s][...], preferred_element_type=jnp.float32)
        total = term if total is None else total + term
    grad_ref[...] = total


def moved_body(codes_ref, *refs):
    *backs, out_ref = refs
    back = backs[0][...]
    for other in backs[1:]:
        back = back + other[...].astype(jnp.float32)
    out_ref[...] = codes_ref[...].astype(jnp.float32) - 0.05 * back.T


def codes_body(moved_ref, back_ref, out_ref):
    moved = moved_ref[...] - 0.05 * back_ref[...].astype(jnp.float32).T
    out_ref[...] = (moved - jnp.clip(moved, -0.02, 0.02)).astype(jnp.bfloat16)


def adam_update(master, moment, second, grad):
    new_moment = 0.9 * moment + 0.1 * grad
    new_second = 0.999 * second + 0.001 * grad * grad
    new_dictionary = master - 0.05 * (new_moment / first_fix) / (
        jnp.sqrt(new_second / second_fix) + 1e-08
    )
    return (new_dictionary, new_moment, new_second)


def iteration(codes, image, master, moment, second):
    rows, cols, atoms = codes.shape
    own_bands, taps = master.shape[0], master.shape[1]
    groups, count, peers = lax.axis_size("row"), lax.axis_size("col"), lax.axis_size("atom")
    bands = groups * own_bands
    reach = taps // 2
    pixels = rows * cols
    ext = -(-(rows + 2 * reach) * cols // 128) * 128
    row_at, col_at = lax.axis_index("row"), lax.axis_index("col")

    assert count == 4
    tile = codes.reshape(pixels, atoms)
    two = along(codes, TWO).reshape(pixels, atoms)
    near = along(codes, NEAR).reshape(pixels, atoms)
    swapped = along(codes, INNER).reshape(pixels, atoms)

    own_filters = jnp.transpose(master, (1, 2, 0, 3)).reshape(taps * taps, own_bands, atoms).astype(jnp.bfloat16)
    filters = [own_filters]
    for s in range(1, groups):
        filters.append(shifted(own_filters, "row", s))
    filters = jnp.concatenate(filters, axis=1).reshape(taps * taps * bands, atoms)
    (turned,) = call(turn_body, [struct(filters.shape[::-1], filters.dtype)], [filters])

    picture = image.reshape(pixels, groups, count, own_bands).transpose(1, 2, 3, 0)
    picture = jnp.stack([lax.dynamic_index_in_dim(picture, (row_at + groups - s) % groups, 0, False) for s in range(groups)])
    pieces = [lax.dynamic_index_in_dim(picture, (col_at + s) % count, 1, False).reshape(bands, pixels) for s in range(count)]
    images = []
    for s in range(count):
        images.append(pieces[s] if s == 0 else shifted(pieces[s], "col", s))

    passed = along(two, [(2, 3), (1, 0)])

    size = struct((bands, ext), jnp.float32)
    y_scratch = [pltpu.VMEM((taps * taps * bands, pixels), jnp.float32)]
    tile_flops = 2 * taps * taps * bands * pixels * atoms
    mains, spills = [], []
    for early in [tile, two, near]:
        body = functools.partial(early_body, taps, bands, ext, cols)
        main, spill = call(body, [size, size], [filters, early], tile_flops, y_scratch)
        mains.append(main)
        spills.append(spill)
    edge = struct((count, bands, 128), jnp.float32)
    part_shape = (count, bands, ext)
    part, far, *edges = call(
        functools.partial(late_body, taps, bands, ext, cols, pixels, 1.0 / peers),
        [struct(part_shape, jnp.float32), struct(tile.shape, tile.dtype)] + [edge] * (1 if groups == 2 else 2),
        [filters, swapped, passed, *mains, *spills, *images],
        tile_flops,
        [pltpu.VMEM(part_shape, jnp.float32)] * 2 + y_scratch,
    )
    if groups == 2:
        edges = [shifted(edges[0], "row", 1)]
    else:
        edges = [moved_on(edges[0], "row", -1), moved_on(edges[1], "row", 1)]
    part, send = call(
        functools.partial(join_body, count, pixels, own_bands),
        [struct(part_shape, jnp.float32), struct(part_shape, jnp.bfloat16)],
        [part, *edges],
    )
    if peers <= 4:
        others = []
        for m in range(peers - 1, 0, -1):
            others.append(lax.ppermute(send, "atom", [(i, i ^ m) for i in range(peers)]))
    else:
        others = [(lax.psum(send, "atom").astype(jnp.float32) - send.astype(jnp.float32)).astype(jnp.bfloat16)]

    def back_of(which, dtypes, *args, peers=None):
        outs = [struct((taps * taps * bands, pixels), jnp.bfloat16)] + [struct((atoms, pixels), dtype) for dtype in dtypes]
        if peers is not None:
            outs.append(struct(part_shape, jnp.float32))
        body = functools.partial(back_body, taps, bands, ext, rows, cols, which, peers)
        return call(body, outs, [turned, *args], tile_flops)

    far_windows, far_back, resid = back_of("far", [jnp.bfloat16], part, *others, peers=len(others))
    home_pass = along(far_back, [(3, 2), (0, 1)])
    home_swap = along(far_back, INNER)
    two_windows, two_back, two_send = back_of("two", [jnp.float32, jnp.bfloat16], resid)
    home_two = along(two_send, TWO[::3])
    near_windows, near_back = back_of("near", [jnp.bfloat16], resid)
    home_near = along(near_back, NEAR)
    own_windows, own_back = back_of("own", [jnp.float32], resid)
    (two_back,) = call(merge_body, [struct((atoms, pixels), jnp.bfloat16)], [two_back, home_pass])
    home_both = along(two_back, TWO[1:3])
    (grad,) = call(
        functools.partial(grad_body, count),
        [struct((taps * taps * bands, atoms), jnp.float32)],
        [own_windows, two_windows, near_windows, far_windows, tile, two, near, far],
        tile_flops * count,
    )
    grad = grad.reshape(taps * taps, groups, own_bands, atoms)
    own_grad = grad[:, 0]
    for s in range(1, groups):
        piece = grad[:, s].astype(jnp.bfloat16)
        piece = shifted(piece, "row", -s)
        own_grad = own_grad + piece.astype(jnp.float32)
    own_grad = jnp.transpose(own_grad.reshape(taps, taps, own_bands, atoms), (2, 0, 1, 3))
    new_dictionary, new_moment, new_second = adam_update(master, moment, second, own_grad)
    (moved,) = call(
        moved_body, [struct((pixels, atoms), jnp.float32)], [tile, own_back, home_near, home_swap, home_two]
    )
    (new_codes,) = call(codes_body, [struct((pixels, atoms), jnp.bfloat16)], [moved, home_both])
    return (new_codes.reshape(rows, cols, atoms), new_dictionary, new_moment, new_second)


def solution(mesh):
    return jax.shard_map(
        iteration,
        mesh=mesh,
        in_specs=(
            P("row", "col", "atom"),
            P("row", "col", None),
            P(("row", "col"), None, None, "atom"),
            P(("row", "col"), None, None, "atom"),
            P(("row", "col"), None, None, "atom"),
        ),
        out_specs=(
            P("row", "col", "atom"),
            P(("row", "col"), None, None, "atom"),
            P(("row", "col"), None, None, "atom"),
            P(("row", "col"), None, None, "atom"),
        ),
        check_vma=False,
    )
```

```python
import functools

import jax
import jax.numpy as jnp
from jax import lax
from jax.experimental import pallas as pl
from jax.experimental.pallas import tpu as pltpu
from jax.sharding import PartitionSpec as P


first_fix = 0.9999734386011124
second_fix = 0.09520785288629038


def shifted(x, axis, step):
    count = lax.axis_size(axis)
    return lax.ppermute(x, axis, [(i, (i + step) % count) for i in range(count)])


def moved_on(x, axis, step):
    count = lax.axis_size(axis)
    return lax.ppermute(x, axis, [(i, i + step) for i in range(count) if 0 <= i + step < count])


TWO = [(0, 2), (1, 3), (2, 0), (3, 1)]
NEAR = [(0, 1), (1, 0), (2, 3), (3, 2)]
INNER = [(1, 2), (2, 1)]


def along(x, pairs):
    return lax.ppermute(x, "col", pairs)


def call(body, outs, args, flops=0, scratch=()):
    moved = sum(a.size * a.dtype.itemsize for a in args) + sum(o.size * o.dtype.itemsize for o in outs)
    return pl.pallas_call(
        body,
        out_shape=outs,
        in_specs=[pl.BlockSpec(memory_space=pltpu.VMEM)] * len(args),
        out_specs=[pl.BlockSpec(memory_space=pltpu.VMEM)] * len(outs),
        scratch_shapes=list(scratch),
        cost_estimate=pl.CostEstimate(flops=flops, bytes_accessed=moved, transcendentals=0),
        compiler_params=pltpu.CompilerParams(vmem_limit_bytes=24 << 20),
    )(*args)


def roll(x, amount):
    amount %= x.shape[1]
    return pltpu.roll(x, amount, 1) if amount else x


def struct(shape, dtype):
    return jax.ShapeDtypeStruct(shape, dtype)


def column_of(ext, cols):
    return lax.broadcasted_iota(jnp.int32, (1, ext), 1) % cols


def tile_parts(filters, tile, y_ref, taps, bands, ext, cols):
    reach = taps // 2
    y_ref[...] = lax.dot_general(filters, tile, (((1,), (1,)), ((), ())), preferred_element_type=jnp.float32)
    pixels = tile.shape[0]
    column = column_of(ext, cols)
    main = jnp.zeros((bands, ext), jnp.float32)
    to_right = jnp.zeros((bands, ext), jnp.float32)
    to_left = jnp.zeros((bands, ext), jnp.float32)
    tail = jnp.zeros((bands, ext - pixels), jnp.float32)
    for b in range(taps):
        total = None
        for a in range(taps):
            term = jnp.concatenate([y_ref[pl.ds((a * taps + b) * bands, bands), :], tail], axis=1)
            total = term if total is None else roll(total, cols) + term
        step = reach - b
        turned = roll(total, step)
        if step > 0:
            inside = column >= step
            to_right = to_right + jnp.where(inside, 0.0, turned)
        elif step < 0:
            inside = column < cols + step
            to_left = to_left + jnp.where(inside, 0.0, turned)
        main = main + (turned if step == 0 else jnp.where(inside, turned, 0.0))
    return main, roll(to_right, -cols) + roll(to_left, cols)


def early_body(taps, bands, ext, cols, filters_ref, tile_ref, main_ref, spill_ref, y_ref):
    main, spill = tile_parts(filters_ref[...], tile_ref[...], y_ref, taps, bands, ext, cols)
    main_ref[...] = main
    spill_ref[...] = spill


def tile_flags(s):
    count = lax.axis_size("col")
    place = lax.rem(lax.axis_index("col") + count - s, count)
    return place > 0, place < count - 1


def near_place():
    return jnp.where(lax.rem(lax.axis_index("col"), 2) == 1, 1, lax.axis_size("col") - 1)


def edges_of(value, pixels, reach, cols, places):
    lane = lax.broadcasted_iota(jnp.int32, (1, 128), 1)
    up = jnp.where(lane < 2 * reach * cols, value[:, :128], 0.0)
    down = value[:, pixels : pixels + 128]
    return [jnp.where(lax.axis_index("row") == 0, down, up)] if places == 1 else [up, down]


def late_body(taps, bands, ext, cols, pixels, *refs):
    filters_ref, swapped_ref, passed_ref = refs[:3]
    mains, spills = refs[3:6], refs[6:9]
    out_ref, tile_ref, *edge_refs, main_of, spill_of, y_ref = refs[9:]
    count, reach = 4, taps // 2
    middle = (lax.axis_index("col") == 1) | (lax.axis_index("col") == 2)
    tile_ref[...] = jnp.where(middle, swapped_ref[...], passed_ref[...])
    near = near_place()
    places = [0, 2, near]
    for s, main, spill in zip(places, mains, spills):
        main_of[s] = main[...]
        spill_of[s] = spill[...]
    main_of[count - near], spill_of[count - near] = tile_parts(filters_ref[...], tile_ref[...], y_ref, taps, bands, ext, cols)
    column = column_of(ext, cols)
    for s in range(count):
        left, right = tile_flags(s)
        from_left = jnp.where((column < reach) & left, spill_of[(s + 1) % count], 0.0)
        from_right = jnp.where((column >= cols - reach) & right, spill_of[(s - 1) % count], 0.0)
        value = main_of[s] + from_left + from_right
        out_ref[s] = value
        for ref, edge in zip(edge_refs, edges_of(value, pixels, reach, cols, len(edge_refs))):
            ref[s] = edge


def frame_body(bands, ext, cols, pixels, reach, *refs):
    images, out_ref, edge_refs = refs[:4], refs[4], refs[5:]
    for s, image in enumerate(images):
        pad = jnp.zeros((bands, ext - pixels), jnp.float32)
        value = roll(jnp.concatenate([image[...].astype(jnp.float32), pad], axis=1), reach * cols)
        out_ref[s] = value
        for ref, edge in zip(edge_refs, edges_of(value, pixels, reach, cols, len(edge_refs))):
            ref[s] = edge


def join_body(count, pixels, turn, edges, *refs):
    part_ref, edge_refs, out_ref, send_refs = refs[0], refs[1 : 1 + edges], refs[1 + edges], refs[2 + edges :]
    bands = part_ref.shape[1]

    def turned(x, step):
        step %= bands
        return x if step == 0 else jnp.concatenate([x[bands - step :], x[: bands - step]], axis=0)

    for s in range(count):
        pieces = [turned(ref[s], turn * sign) for ref, sign in zip(edge_refs, (-1, 1))]
        if len(pieces) == 1:
            first = lax.axis_index("row") == 0
            pieces = [jnp.where(first, pieces[0], 0.0), jnp.where(first, 0.0, pieces[0])]
        below, above = pieces
        own = part_ref[s]
        parts = [own[:, :128] + above, own[:, 128:pixels], own[:, pixels : pixels + 128] + below, own[:, pixels + 128 :]]
        value = jnp.concatenate([part for part in parts if part.shape[1]], axis=1)
        out_ref[s] = value
        for send_ref in send_refs:
            send_ref[s] = value.astype(jnp.bfloat16)


def resid_body(ext, rows, cols, reach, peers, *refs):
    image_ref, own_ref, others, out_ref = refs[0], refs[1], refs[2 : 2 + peers], refs[2 + peers]
    line = lax.broadcasted_iota(jnp.int32, (1, ext), 1) // cols
    place, places = lax.axis_index("row"), lax.axis_size("row")
    real = ((line >= reach) | (place > 0)) & ((line < rows + reach) | (place < places - 1)) & (line < rows + 2 * reach)
    for s in range(out_ref.shape[0]):
        value = own_ref[s]
        for other in others:
            value = value + other[s].astype(jnp.float32)
        out_ref[s] = jnp.where(real, value - image_ref[s], 0.0).astype(jnp.bfloat16).astype(jnp.float32)


def windows_of(taps, bands, ext, rows, cols, s, resid_ref, windows_ref):
    reach = taps // 2
    pixels = rows * cols
    count = resid_ref.shape[0]
    column = column_of(ext, cols)
    left, right = tile_flags(s)
    own = resid_ref[s]
    to_left = jnp.where(left, resid_ref[lax.rem(s + 1, count)], 0.0)
    to_right = jnp.where(right, resid_ref[lax.rem(s + count - 1, count)], 0.0)
    for b in range(taps):
        step = b - reach
        if step == 0:
            view = own
        elif step > 0:
            view = jnp.where(column >= step, roll(own, step), roll(to_left, step - cols))
        else:
            view = jnp.where(column < cols + step, roll(own, step), roll(to_right, step + cols))
        for a in range(taps):
            part = roll(view, -cols * (2 * reach - a))[:, :pixels]
            at = (a * taps + b) * bands
            windows_ref[at : at + bands, :] = part.astype(jnp.bfloat16)


def back_body(taps, bands, ext, rows, cols, which, peers, *refs):
    near = near_place()
    s = {"own": 0, "two": 2, "near": near, "far": 4 - near}[which]
    turned_ref = refs[0]
    if peers is None:
        resid_ref, (windows_ref, *back_refs) = refs[1], refs[2:]
    else:
        windows_ref, *back_refs, resid_ref = refs[-3:]
        resid_body(ext, rows, cols, taps // 2, peers, *refs[1:-3], resid_ref)
    windows_of(taps, bands, ext, rows, cols, s, resid_ref, windows_ref)
    back = jnp.dot(turned_ref[...], windows_ref[...], preferred_element_type=jnp.float32)
    for back_ref in back_refs:
        back_ref[...] = back.astype(back_ref.dtype)


def merge_body(back_ref, passed_ref, out_ref):
    out_ref[...] = (back_ref[...] + passed_ref[...].astype(jnp.float32)).astype(jnp.bfloat16)


def turn_body(filters_ref, out_ref):
    out_ref[...] = filters_ref[...].T


def grad_body(count, *refs):
    windows, tiles, grad_ref = refs[:count], refs[count : 2 * count], refs[2 * count]
    total = None
    for s in range(count):
        term = jnp.dot(windows[s][...], tiles[s][...], preferred_element_type=jnp.float32)
        total = term if total is None else total + term
    grad_ref[...] = total


def moved_body(codes_ref, *refs):
    *backs, out_ref = refs
    back = backs[0][...]
    for other in backs[1:]:
        back = back + other[...].astype(jnp.float32)
    out_ref[...] = codes_ref[...].astype(jnp.float32) - 0.05 * back.T


def codes_body(moved_ref, back_ref, out_ref):
    moved = moved_ref[...] - 0.05 * back_ref[...].astype(jnp.float32).T
    out_ref[...] = (moved - jnp.clip(moved, -0.02, 0.02)).astype(jnp.bfloat16)


def adam_update(master, moment, second, grad):
    new_moment = 0.9 * moment + 0.1 * grad
    new_second = 0.999 * second + 0.001 * grad * grad
    new_dictionary = master - 0.05 * (new_moment / first_fix) / (
        jnp.sqrt(new_second / second_fix) + 1e-08
    )
    return (new_dictionary, new_moment, new_second)


def iteration(codes, image, master, moment, second):
    rows, cols, atoms = codes.shape
    own_bands, taps = master.shape[0], master.shape[1]
    groups, count, peers = lax.axis_size("row"), lax.axis_size("col"), lax.axis_size("atom")
    bands = groups * own_bands
    reach = taps // 2
    pixels = rows * cols
    ext = -(-(rows + 2 * reach) * cols // 128) * 128
    row_at, col_at = lax.axis_index("row"), lax.axis_index("col")

    assert count == 4
    tile = codes.reshape(pixels, atoms)
    two = along(codes, TWO).reshape(pixels, atoms)
    near = along(codes, NEAR).reshape(pixels, atoms)
    swapped = along(codes, INNER).reshape(pixels, atoms)

    own_filters = jnp.transpose(master, (1, 2, 0, 3)).reshape(taps * taps, own_bands, atoms).astype(jnp.bfloat16)
    filters = [own_filters]
    for s in range(1, groups):
        filters.append(shifted(own_filters, "row", s))
    filters = jnp.concatenate(filters, axis=1).reshape(taps * taps * bands, atoms)
    (turned,) = call(turn_body, [struct(filters.shape[::-1], filters.dtype)], [filters])

    picture = image.reshape(pixels, groups, count, own_bands).transpose(1, 2, 3, 0)
    picture = jnp.stack([lax.dynamic_index_in_dim(picture, (row_at + groups - s) % groups, 0, False) for s in range(groups)])
    pieces = [lax.dynamic_index_in_dim(picture, (col_at + s) % count, 1, False).reshape(bands, pixels) for s in range(count)]
    images = []
    for s in range(count):
        images.append(pieces[s] if s == 0 else shifted(pieces[s], "col", s))

    passed = along(two, [(2, 3), (1, 0)])

    size = struct((bands, ext), jnp.float32)
    y_scratch = [pltpu.VMEM((taps * taps * bands, pixels), jnp.float32)]
    tile_flops = 2 * taps * taps * bands * pixels * atoms
    mains, spills = [], []
    for early in [tile, two, near]:
        body = functools.partial(early_body, taps, bands, ext, cols)
        main, spill = call(body, [size, size], [filters, early], tile_flops, y_scratch)
        mains.append(main)
        spills.append(spill)
    edge = struct((count, bands, 128), jnp.float32)
    part_shape = (count, bands, ext)
    part, far, *edges = call(
        functools.partial(late_body, taps, bands, ext, cols, pixels),
        [struct(part_shape, jnp.float32), struct(tile.shape, tile.dtype)] + [edge] * (1 if groups == 2 else 2),
        [filters, swapped, passed, *mains, *spills],
        tile_flops,
        [pltpu.VMEM(part_shape, jnp.float32)] * 2 + y_scratch,
    )
    edges_out = 1 if groups == 2 else 2

    def whole_rows(part, edges, sends):
        if groups == 2:
            edges = [shifted(edges[0], "row", 1)]
        else:
            edges = [moved_on(edges[0], "row", -1), moved_on(edges[1], "row", 1)]
        return call(
            functools.partial(join_body, count, pixels, own_bands, edges_out),
            [struct(part_shape, jnp.float32)] + [struct(part_shape, jnp.bfloat16)] * sends,
            [part, *edges],
        )

    part, send = whole_rows(part, edges, 1)
    if peers <= 4:
        others = []
        for m in range(peers - 1, 0, -1):
            others.append(lax.ppermute(send, "atom", [(i, i ^ m) for i in range(peers)]))
    else:
        others = [(lax.psum(send, "atom").astype(jnp.float32) - send.astype(jnp.float32)).astype(jnp.bfloat16)]

    picture, *edges = call(
        functools.partial(frame_body, bands, ext, cols, pixels, reach),
        [struct(part_shape, jnp.float32)] + [edge] * edges_out,
        images,
    )
    (picture,) = whole_rows(picture, edges, 0)

    def back_of(which, dtypes, *args, peers=None):
        outs = [struct((taps * taps * bands, pixels), jnp.bfloat16)] + [struct((atoms, pixels), dtype) for dtype in dtypes]
        if peers is not None:
            outs.append(struct(part_shape, jnp.float32))
        body = functools.partial(back_body, taps, bands, ext, rows, cols, which, peers)
        return call(body, outs, [turned, *args], tile_flops)

    far_windows, far_back, resid = back_of("far", [jnp.bfloat16], picture, part, *others, peers=len(others))
    home_pass = along(far_back, [(3, 2), (0, 1)])
    home_swap = along(far_back, INNER)
    two_windows, two_back, two_send = back_of("two", [jnp.float32, jnp.bfloat16], resid)
    home_two = along(two_send, TWO[::3])
    near_windows, near_back = back_of("near", [jnp.bfloat16], resid)
    home_near = along(near_back, NEAR)
    own_windows, own_back = back_of("own", [jnp.float32], resid)
    (two_back,) = call(merge_body, [struct((atoms, pixels), jnp.bfloat16)], [two_back, home_pass])
    home_both = along(two_back, TWO[1:3])
    (grad,) = call(
        functools.partial(grad_body, count),
        [struct((taps * taps * bands, atoms), jnp.float32)],
        [own_windows, two_windows, near_windows, far_windows, tile, two, near, far],
        tile_flops * count,
    )
    grad = grad.reshape(taps * taps, groups, own_bands, atoms)
    own_grad = grad[:, 0]
    for s in range(1, groups):
        piece = grad[:, s].astype(jnp.bfloat16)
        piece = shifted(piece, "row", -s)
        own_grad = own_grad + piece.astype(jnp.float32)
    own_grad = jnp.transpose(own_grad.reshape(taps, taps, own_bands, atoms), (2, 0, 1, 3))
    new_dictionary, new_moment, new_second = adam_update(master, moment, second, own_grad)
    (moved,) = call(
        moved_body, [struct((pixels, atoms), jnp.float32)], [tile, own_back, home_near, home_swap, home_two]
    )
    (new_codes,) = call(codes_body, [struct((pixels, atoms), jnp.bfloat16)], [moved, home_both])
    return (new_codes.reshape(rows, cols, atoms), new_dictionary, new_moment, new_second)


def solution(mesh):
    return jax.shard_map(
        iteration,
        mesh=mesh,
        in_specs=(
            P("row", "col", "atom"),
            P("row", "col", None),
            P(("row", "col"), None, None, "atom"),
            P(("row", "col"), None, None, "atom"),
            P(("row", "col"), None, None, "atom"),
        ),
        out_specs=(
            P("row", "col", "atom"),
            P(("row", "col"), None, None, "atom"),
            P(("row", "col"), None, None, "atom"),
            P(("row", "col"), None, None, "atom"),
        ),
        check_vma=False,
    )
```
